32 devices in a mesh: dp: 4 (over y, x), fsdp: 8 (over z, core).
Axes of the slice: x: 2, y: 2, z: 4, core: 2. Of those that a mesh axis runs over, the one named last changes fastest.
Arguments:
- hidden: bfloat16 [2, 4608, 4096], P(None, ('dp', 'fsdp')), may hold values from -120 to 120
- cotangent: bfloat16 [2, 4608, 1024], P(None, ('dp', 'fsdp')), may hold values from -6 to 6
- proj_weight: bfloat16 [2, 4096, 1024], P(None, 'fsdp'), may hold values from -3 to 3
- norm_gain: float32 [2, 4096], replicated, may hold values from 0.1 to 1.9
- prev_factor: bfloat16 [2, 512, 128], replicated, may hold values from -0.25 to 0.25
- factor_ranks: int32 [2, 2], replicated, may hold values from 4 to 64, as said below
- layer_order: int32 [2], replicated, may hold values from 0 to 1, each once
Outputs:
- hidden_grad: bfloat16 [4608, 4096], P(('dp', 'fsdp'))
- basis_factor: float32 [2, 4096, 128], P(None, 'fsdp')
The draws below stay inside these ranges and needn't reach their ends.
Inputs may be any that keep to these rules, and one draw needn't show every extreme that they name: `factor_ranks`: every draw holds a rank equal to 64 and a rank equal to 4.
All inputs are finite; a program needn't handle non-finite values.
Results may differ from the reference program's by a relative error of at most 0.0056.
Values may be sent and summed in bfloat16 or wider, within the bound.
A program may use at most 64 MiB of HBM per device.

```python
import math
import jax
import jax.numpy as jnp
from jax import lax

D = 4096
KVW = 512
RMAX = 64
LAYERS = 2
TOK_DEV = 144
TOKENS = 4608
N_DP = 4
N_FSDP = 8


def shared_direction(key):
    shared_key = jax.random.fold_in(key, 29)
    shared = jnp.clip(jax.random.normal(shared_key, (LAYERS, D), jnp.float32), -3.0, 3.0)
    feature = jnp.arange(D, dtype=jnp.float32) / D
    rising = jnp.exp(jnp.log(3.0) * feature)
    return (shared, rising)


def draw_hidden(key, part):
    first_key = jax.random.fold_in(jax.random.fold_in(key, 5), 0)
    shared, rising = shared_direction(key)
    base_values = jnp.clip(jax.random.normal(first_key, (LAYERS, TOKENS, D), jnp.float32), -6.0, 6.0)
    values = base_values + 0.6 * shared[:, None, :]
    return (values * rising[None, None, :]).astype(jnp.bfloat16)


def draw_proj_weight(key, part):
    shared, rising = shared_direction(key)
    base_key = jax.random.fold_in(key, 13)
    column_key = jax.random.fold_in(key, 17)
    fan_scale = (2.0 * KVW) ** (-0.5)
    base_values = jnp.clip(jax.random.normal(base_key, (LAYERS, D, 2 * KVW), jnp.float32), -6.0, 6.0) * fan_scale
    column = jnp.clip(jax.random.normal(column_key, (LAYERS, 2 * KVW), jnp.float32), -3.0, 3.0)
    aligned = (shared * rising[None, :])[:, :, None] * column[:, None, :]
    values = base_values + 0.5 * fan_scale * aligned
    return values.astype(jnp.bfloat16)


def draw_factor_ranks(key, part):
    first_key, second_key = jax.random.split(jax.random.fold_in(key, 11))
    values = jax.random.randint(first_key, (LAYERS * 2,), 4, RMAX + 1)
    places = jax.random.permutation(second_key, LAYERS * 2)
    values = values.at[places[0]].set(RMAX).at[places[1]].set(4)
    return values.reshape(LAYERS, 2).astype(jnp.int32)


def block_scale(key, shape, shards, low, top_value):
    gain, own = 1.0, jax.random.fold_in(key, 6)
    for dim, blocks in shards:
        steps = jnp.exp(jax.random.uniform(jax.random.fold_in(own, dim), (blocks,), jnp.float32, low / len(shards), top_value / len(shards)))
        gain = gain * jnp.repeat(steps, shape[dim] // blocks).reshape([-1 if axis == dim else 1 for axis in range(len(shape))])
    return gain


def centred(key, extent, width, bound, shards=(), held_as=jnp.bfloat16):
    entries = jax.random.normal(key, extent, jnp.float32) * width
    if len(shards) > 0:
        entries = block_scale(key, extent, shards, -0.22, 0.18) * entries
    return jnp.clip(entries, min=-bound, max=bound).astype(held_as)


def setup_inputs(seed: int = 0) -> dict:
    keys = jax.random.split(jax.random.key(seed), 8)
    return {
        "hidden": draw_hidden(jax.random.fold_in(keys[7], 71), 0),
        "cotangent": centred(keys[1], (LAYERS, TOKENS, 2 * KVW), 1.0, 6.0, ((1, 32),)),
        "proj_weight": draw_proj_weight(jax.random.fold_in(keys[7], 71), 0),
        "norm_gain": jnp.clip(1.0 + 0.18 * jax.random.normal(keys[3], (LAYERS, D), jnp.float32), 0.1, 1.9),
        "prev_factor": centred(keys[4], (LAYERS, KVW, 2 * RMAX), KVW ** -0.5, 0.25),
        "factor_ranks": draw_factor_ranks(jax.random.fold_in(keys[7], 71), 0),
        "layer_order": jax.random.permutation(keys[6], LAYERS).astype(jnp.int32),
    }


def normalize(hidden_rows, gain_row):
    wide_rows = hidden_rows.astype(jnp.float32)
    inverse = lax.rsqrt(lax.optimization_barrier(jnp.mean(wide_rows * wide_rows, axis=1, keepdims=True)) + 1e-05)
    normed = (wide_rows * inverse * gain_row[None, :]).astype(jnp.bfloat16)
    return (inverse, normed)

def masked_factors(factors, rank_pair):
    rank_cols = factors.shape[1] // 2
    position = jnp.arange(2 * rank_cols)
    column = position % rank_cols
    column_limit = jnp.where(position < rank_cols, rank_pair[0], rank_pair[1])
    return jnp.where((column < column_limit)[None, :], factors, jnp.zeros_like(factors))

def project(grad_rows, kept_factor):
    head_cols = grad_rows.shape[1] // 2
    rank_cols = kept_factor.shape[1] // 2
    keys_part = jnp.dot(grad_rows[:, :head_cols].astype(jnp.float32), kept_factor[:, :rank_cols].astype(jnp.float32), preferred_element_type=jnp.float32)
    values_part = jnp.dot(grad_rows[:, head_cols:].astype(jnp.float32), kept_factor[:, rank_cols:].astype(jnp.float32), preferred_element_type=jnp.float32)
    return jnp.concatenate([keys_part, values_part], axis=1).astype(jnp.bfloat16)

def gram_pair(factor_rows):
    row_count = factor_rows.shape[0]
    rank_cols = factor_rows.shape[1] // 2
    paired = factor_rows.reshape(row_count, 2, rank_cols)
    return jnp.einsum('rmi,rmj->mij', paired.astype(jnp.float32), paired.astype(jnp.float32), precision=lax.Precision.HIGHEST, preferred_element_type=jnp.float32)

def orthonormal(factor_rows, gram_totals, rank_pair):
    rank_cols = factor_rows.shape[1] // 2
    column = jnp.arange(rank_cols)
    pieces = []
    for member in range(2):
        block_cols = factor_rows[:, member * rank_cols:(member + 1) * rank_cols]
        padded = gram_totals[member] + jnp.diag((column >= rank_pair[member]).astype(gram_totals.dtype))
        lower_factor = jnp.linalg.cholesky(padded)
        pieces.append(lax.linalg.triangular_solve(lower_factor, block_cols, left_side=False, lower=True, transpose_a=True))
    return math.sqrt(D) * jnp.concatenate(pieces, axis=1)

def reference(hidden, cotangent, proj_weight, norm_gain, prev_factor, factor_ranks, layer_order):
    block_rows = TOK_DEV * N_FSDP
    block_count = N_DP
    basis_list = []
    for slot_index in range(LAYERS):
        kept_factor = masked_factors(prev_factor[slot_index], factor_ranks[slot_index])
        hidden_blocks = hidden[slot_index].reshape(block_count, block_rows, D)
        grad_blocks = cotangent[slot_index].reshape(block_count, block_rows, 2 * KVW)
        gain_row = norm_gain[slot_index]

        def accumulate(running, paired_rows):
            hidden_rows, grad_rows = paired_rows
            inverse, normed = normalize(hidden_rows, gain_row)
            projected = project(grad_rows, kept_factor)
            return (running + jnp.dot(normed.T.astype(jnp.float32), projected.astype(jnp.float32), preferred_element_type=jnp.float32), None)
        summed_factor, unused = lax.scan(accumulate, jnp.zeros((D, 2 * RMAX), jnp.float32), (hidden_blocks, grad_blocks))
        basis_list.append(orthonormal(summed_factor, gram_pair(summed_factor), factor_ranks[slot_index]))
    top_slot = layer_order[0]
    top_weight = lax.dynamic_index_in_dim(proj_weight, top_slot, 0, keepdims=False)
    top_gain = lax.dynamic_index_in_dim(norm_gain, top_slot, 0, keepdims=False)
    top_hidden = lax.dynamic_index_in_dim(hidden, top_slot, 0, keepdims=False).reshape(block_count, block_rows, D)
    top_grads = lax.dynamic_index_in_dim(cotangent, top_slot, 0, keepdims=False).reshape(block_count, block_rows, 2 * KVW)

    def backward_block(paired_rows):
        hidden_rows, grad_rows = paired_rows
        inverse, normed = normalize(hidden_rows, top_gain)
        input_grad = jnp.dot(grad_rows.astype(jnp.float32), top_weight.T.astype(jnp.float32), preferred_element_type=jnp.float32)
        scaled = input_grad * top_gain[None, :]
        unit_rows = hidden_rows.astype(jnp.float32) * inverse
        inner_mean = lax.optimization_barrier(jnp.mean(scaled * unit_rows, axis=1, keepdims=True))
        return (inverse * (scaled - unit_rows * inner_mean)).astype(jnp.bfloat16)
    hidden_grad = lax.map(backward_block, (top_hidden, top_grads)).reshape(TOKENS, D)
    return (hidden_grad, jnp.stack(basis_list))
```

```python
import functools
import math

import jax
import jax.numpy as jnp
from jax import lax
from jax.experimental import pallas as pl
from jax.experimental.pallas import tpu as pltpu
from jax.sharding import PartitionSpec as P

D = 4096


def normalize(hidden_rows, gain_row):
    wide_rows = hidden_rows.astype(jnp.float32)
    inverse = lax.rsqrt(jnp.mean(wide_rows * wide_rows, axis=1, keepdims=True) + 1e-05)
    normed = (wide_rows * inverse * gain_row[None, :]).astype(jnp.bfloat16)
    return (inverse, normed)


def masked_factors(factors, rank_pair):
    rank_cols = factors.shape[1] // 2
    position = jnp.arange(2 * rank_cols)
    column = position % rank_cols
    column_limit = jnp.where(position < rank_cols, rank_pair[0], rank_pair[1])
    return jnp.where((column < column_limit)[None, :], factors, jnp.zeros_like(factors))


def project(grad_rows, kept_factor):
    head_cols = grad_rows.shape[1] // 2
    rank_cols = kept_factor.shape[1] // 2
    keys_part = jnp.dot(
        grad_rows[:, :head_cols], kept_factor[:, :rank_cols], preferred_element_type=jnp.float32
    )
    values_part = jnp.dot(
        grad_rows[:, head_cols:], kept_factor[:, rank_cols:], preferred_element_type=jnp.float32
    )
    return jnp.concatenate([keys_part, values_part], axis=1).astype(jnp.bfloat16)


def gram_pair(factor_shard):
    row_count = factor_shard.shape[0]
    rank_cols = factor_shard.shape[1] // 2
    paired = factor_shard.reshape(row_count, 2, rank_cols)
    return jnp.einsum(
        "rmi,rmj->mij",
        paired,
        paired,
        precision=lax.Precision.HIGHEST,
        preferred_element_type=jnp.float32,
    )


def orthonormal(factor_shard, gram_totals, rank_pair):
    rank_cols = factor_shard.shape[1] // 2
    column = jnp.arange(rank_cols)
    pieces = []
    for member in range(2):
        block_cols = factor_shard[:, member * rank_cols : (member + 1) * rank_cols]
        padded = gram_totals[member] + jnp.diag((column >= rank_pair[member]).astype(jnp.float32))
        lower_factor = jnp.linalg.cholesky(padded)
        pieces.append(
            lax.linalg.triangular_solve(
                lower_factor, block_cols, left_side=False, lower=True, transpose_a=True
            )
        )
    return math.sqrt(D) * jnp.concatenate(pieces, axis=1)


def body(hidden, cotangent, proj_weight, norm_gain, prev_factor, factor_ranks, layer_order):
    layer_count = hidden.shape[0]
    top_slot = layer_order[0]
    inverses = []
    shards = []
    basis_list = []
    for slot_index in range(layer_count):
        inverse, normed = normalize(hidden[slot_index], norm_gain[slot_index])
        inverses.append(inverse)
        kept_factor = masked_factors(prev_factor[slot_index], factor_ranks[slot_index])
        projected = project(cotangent[slot_index], kept_factor)
        local_rows = lax.psum_scatter(
            lax.dot_general(
                normed, projected, (((0,), (0,)), ((), ())), preferred_element_type=jnp.float32
            ),
            "fsdp",
            scatter_dimension=0,
            tiled=True,
        )
        factor_shard = lax.psum(local_rows, "dp")
        shards.append(factor_shard)
    stacked = jnp.stack([gram_pair(factor_shard) for factor_shard in shards])
    all_grams = lax.psum(stacked, "fsdp")
    basis_list = [
        orthonormal(shards[slot_index], all_grams[slot_index], factor_ranks[slot_index])
        for slot_index in range(layer_count)
    ]
    top_grads = lax.dynamic_index_in_dim(cotangent, top_slot, 0, keepdims=False)
    top_weight = lax.dynamic_index_in_dim(proj_weight, top_slot, 0, keepdims=False)
    input_grad = lax.dot_general(
        top_grads,
        lax.all_gather(top_weight, "fsdp", axis=0, tiled=True),
        (((1,), (1,)), ((), ())),
        preferred_element_type=jnp.float32,
    )
    top_inverse = lax.dynamic_index_in_dim(jnp.stack(inverses), top_slot, 0, keepdims=False)
    top_gain = lax.dynamic_index_in_dim(norm_gain, top_slot, 0, keepdims=False)
    top_hidden = lax.dynamic_index_in_dim(hidden, top_slot, 0, keepdims=False).astype(jnp.float32)
    scaled = input_grad * top_gain[None, :]
    unit_rows = top_hidden * top_inverse
    inner_mean = jnp.mean(scaled * unit_rows, axis=1, keepdims=True)
    hidden_grad = (top_inverse * (scaled - unit_rows * inner_mean)).astype(jnp.bfloat16)
    return (hidden_grad, jnp.stack(basis_list))


MESH = pl.DeviceIdType.MESH


def fused_kernel(
    n_z, ranks_ref, order_ref, hidden_ref, cot_ref, weight_ref, gain_ref, factor_ref,
    grad_ref, basis_ref,
    acc, s0_send, s0_recv, s1_send, s1_recv, s2_send, s2_recv, keep2, s3_send, s3_recv,
    f_send, f_all, g_all, z_send, z_all, l_send, l_recv, w_all, scaled, inverse,
    send_sem, recv_sem, f_sem, w_send, w_recv, sib_sem, own_sem,
):
    q = lax.axis_index("dp")
    me = lax.axis_index("fsdp")
    z, c = me // 2, me % 2
    y, x = q // 2, q % 2
    n_dp = 4
    width = hidden_ref.shape[2]
    tokens = hidden_ref.shape[1]
    per_z = width // n_z
    heads = cot_ref.shape[2] // 2
    qrows = weight_ref.shape[1]
    half_rows = qrows // 2
    x_nbr = y * 2 + (1 - x)
    y_nbr = (1 - y) * 2 + x
    diag = (1 - y) * 2 + (1 - x)
    sibling = (q, z * 2 + (1 - c))

    def same_core(dp_index, z_index):
        return (dp_index, z_index * 2 + c)

    barrier = pltpu.get_barrier_semaphore()
    peers = [sibling]
    for k in range(1, n_dp):
        for core in range(2):
            peers.append(((q + k) % n_dp, z * 2 + core))
    for d in range(1, n_z):
        peers.append(same_core(q, (z + d) % n_z))
    for peer in peers:
        pl.semaphore_signal(barrier, inc=1, device_id=peer, device_id_type=MESH)
    pl.semaphore_wait(barrier, len(peers))

    pending = []

    def send(src, dst, ssem, rsem, target):
        copy = pltpu.make_async_remote_copy(
            src_ref=src, dst_ref=dst, send_sem=ssem, recv_sem=rsem,
            device_id=target, device_id_type=MESH,
        )
        copy.start()
        pending.append(copy)
        return copy

    def arrived(dst, rsem):
        pltpu.make_async_remote_copy(
            src_ref=dst, dst_ref=dst, send_sem=rsem, recv_sem=rsem,
            device_id=sibling, device_id_type=MESH,
        ).wait_recv()

    def piece(dp_index, z_index, offset, rows):
        start = (z_index * 2 + c) * (n_dp * qrows) + dp_index * qrows + offset
        return w_all.at[pl.ds(pl.multiple_of(start, half_rows), rows)]

    w_count = [0]

    def w_copy(src, dst, rsem, target):
        send(src, dst, w_send.at[w_count[0]], rsem, target)
        w_count[0] += 1

    for d in range(1, n_z):
        w_copy(weight_ref.at[q], piece(q, z, 0, qrows), w_recv.at[0, d - 1], same_core(q, (z + d) % n_z))
    own_copies = []
    for k in range(n_dp):
        own = pltpu.make_async_copy(weight_ref.at[k], piece(k, z, 0, qrows), own_sem.at[k])
        own.start()
        own_copies.append(own)

    lane = lax.broadcasted_iota(jnp.int32, (1, 128), 1)

    def slot_sums(slot, store):
        limit = jnp.where(lane < 64, ranks_ref[2 * slot], ranks_ref[2 * slot + 1])
        kept = jnp.where(lane % 64 < limit, factor_ref[slot].astype(jnp.float32), 0.0).astype(jnp.bfloat16)
        keys_part = jnp.dot(cot_ref[slot, :, :heads], kept, preferred_element_type=jnp.float32)
        values_part = jnp.dot(cot_ref[slot, :, heads:], kept, preferred_element_type=jnp.float32)
        projected = jnp.where(lane < 64, keys_part, values_part).astype(jnp.bfloat16)
        total = jnp.zeros((tokens, 1), jnp.float32)
        for part in range(n_z):
            wide = hidden_ref[slot, :, part * per_z : (part + 1) * per_z].astype(jnp.float32)
            total += jnp.sum(wide * wide, axis=1, keepdims=True)
        inv = lax.rsqrt(total / width + 1e-05)
        inverse[slot] = inv
        flipped = projected.astype(jnp.float32).T.astype(jnp.bfloat16)
        for part in range(n_z):
            cols = slice(part * per_z, (part + 1) * per_z)
            wide = hidden_ref[slot, :, cols].astype(jnp.float32)
            gain = gain_ref[pl.ds(slot, 1), cols]
            normed = (wide * inv * gain).astype(jnp.bfloat16)
            sums = jnp.dot(flipped, normed, preferred_element_type=jnp.float32)
            for yy in range(2):
                for xx in range(2):
                    for h in range(2):
                        first, second = (xx, yy) if h == 0 else (yy, xx)
                        at = (yy * 2 + xx) * 256 + h * 128
                        store(h, first, second, part, sums[:, at : at + 128])

    def store_other(h, first, second, part, block):
        s0_send[h, first, second, part] = block.astype(jnp.bfloat16)

    def store_mine(h, first, second, part, block):
        acc[h, first, second, part] = block

    slot_sums(1 - c, store_other)
    for h in range(2):
        send(s0_send.at[h], s0_recv.at[h], send_sem.at[h], recv_sem.at[h], sibling)
    slot_sums(c, store_mine)

    firsts, seconds = (x, y), (y, x)
    first_nbr, second_nbr = (x_nbr, y_nbr), (y_nbr, x_nbr)
    for h in range(2):
        a = firsts[h]
        arrived(s0_recv.at[h], recv_sem.at[h])
        s1_send[h] = (acc[h, 1 - a] + s0_recv[h, 1 - a].astype(jnp.float32)).astype(jnp.bfloat16)
        send(s1_send.at[h], s1_recv.at[h], send_sem.at[2 + h], recv_sem.at[2 + h], same_core(first_nbr[h], z))
    for h in range(2):
        a = firsts[h]
        acc[h, a] = acc[h, a] + s0_recv[h, a].astype(jnp.float32)
    for h in range(2):
        a, b = firsts[h], seconds[h]
        arrived(s1_recv.at[h], recv_sem.at[2 + h])
        s2_send[h] = (acc[h, a, 1 - b] + s1_recv[h, 1 - b].astype(jnp.float32)).astype(jnp.bfloat16)
        send(s2_send.at[h], s2_recv.at[h], send_sem.at[4 + h], recv_sem.at[4 + h], same_core(second_nbr[h], z))
    for h in range(2):
        a, b = firsts[h], seconds[h]
        keep2[h] = acc[h, a, b] + s1_recv[h, b].astype(jnp.float32)
    for h in range(2):
        arrived(s2_recv.at[h], recv_sem.at[4 + h])
        summed = keep2[h] + s2_recv[h].astype(jnp.float32)
        keep2[h] = summed
        for part in range(n_z):
            s3_send[part, h] = summed[part].astype(jnp.bfloat16)
    for d in range(1, n_z):
        to = (z + d) % n_z
        send(s3_send.at[to], s3_recv.at[z], send_sem.at[5 + d], recv_sem.at[5 + d], same_core(q, to))
    finals = [keep2[h, z] for h in range(2)]
    for d in range(1, n_z):
        source = (z + n_z - d) % n_z
        arrived(s3_recv.at[source], recv_sem.at[5 + d])
        for h in range(2):
            finals[h] = finals[h] + s3_recv[source, h].astype(jnp.float32)

    gram = jnp.zeros((128, 128), jnp.float32)
    for h in range(2):
        gram += lax.dot_general(
            finals[h], finals[h], (((1,), (1,)), ((), ())),
            precision=lax.Precision.HIGHEST, preferred_element_type=jnp.float32,
        )
    g_all[q] = jnp.where(lane < 64, gram[0:64, :], gram[64:128, :])
    for k in range(1, n_dp):
        send(g_all.at[q], g_all.at[q], send_sem.at[8 + k], recv_sem.at[8 + k], same_core((q + k) % n_dp, z))

    for h in range(2):
        f_send[h] = finals[h].astype(jnp.bfloat16)
    f_dst = f_all.at[c, x]
    for k in range(1, n_dp):
        send(f_send, f_dst, send_sem.at[12 + k], f_sem.at[c, x], ((q + k) % n_dp, z * 2 + y))
    local = pltpu.make_async_copy(f_send, f_dst, f_sem.at[c, x])
    to_sibling = pltpu.make_async_remote_copy(
        src_ref=f_send, dst_ref=f_dst, send_sem=send_sem.at[16], recv_sem=f_sem.at[c, x],
        device_id=sibling, device_id_type=MESH,
    )

    @pl.when(y == c)
    def _():
        local.start()

    @pl.when(y != c)
    def _():
        to_sibling.start()

    for own in own_copies:
        own.wait()
    for k in range(n_dp):
        w_copy(weight_ref.at[k], piece(k, z, 0, qrows), sib_sem, sibling)
    for d in range(1, n_z):
        source = (z + n_z - d) % n_z
        block = piece(q, source, 0, qrows)
        arrived(block, w_recv.at[0, d - 1])
        w_copy(block, block, w_recv.at[1, d - 1], same_core(x_nbr, z))
        w_copy(block, block, w_recv.at[2, d - 1], same_core(y_nbr, z))
        w_copy(block, block, sib_sem, sibling)

    def relay(d):
        source = (z + n_z - d) % n_z
        for kind, origin, onward, offset in ((1, x_nbr, y_nbr, 0), (2, y_nbr, x_nbr, half_rows)):
            block = piece(origin, source, 0, qrows)
            arrived(block, w_recv.at[kind, d - 1])
            part = piece(origin, source, offset, half_rows)
            w_copy(part, part, w_recv.at[2 + kind, d - 1], same_core(onward, z))
            w_copy(block, block, sib_sem, sibling)

    for k in range(1, n_dp):
        source = (q + n_dp - k) % n_dp
        arrived(g_all.at[source], recv_sem.at[8 + k])
    plane = g_all[0] + g_all[1] + g_all[2] + g_all[3]
    z_all[z] = plane
    for d in range(1, n_z):
        send(z_all.at[z], z_all.at[z], send_sem.at[16 + d], recv_sem.at[16 + d], same_core(q, (z + d) % n_z))
    for d in range(1, n_z):
        arrived(z_all.at[(z + n_z - d) % n_z], recv_sem.at[16 + d])
    matrix = z_all[0]
    for part in range(1, n_z):
        matrix += z_all[part]

    row = lax.broadcasted_iota(jnp.int32, (64, 128), 0)
    column = lax.broadcasted_iota(jnp.int32, (64, 128), 1)
    left = column < 64
    limit = jnp.where(left, ranks_ref[2 * c], ranks_ref[2 * c + 1])
    on_diagonal = row == column % 64
    matrix = matrix + jnp.where(on_diagonal & (row >= limit), 1.0, 0.0)
    unit = jnp.where(on_diagonal, 1.0, 0.0)
    for j in range(64):
        pivot_row = matrix[j : j + 1, :]
        pivot = jnp.where(lane < 64, matrix[j : j + 1, j : j + 1], matrix[j : j + 1, 64 + j : 65 + j])
        scale = 1.0 / pivot
        factor = jnp.where(left, matrix[:, j : j + 1], matrix[:, 64 + j : 65 + j])
        factor = jnp.where(row > j, factor, 0.0)
        unit_row = unit[j : j + 1, :]
        matrix = matrix - factor * (pivot_row * scale)
        unit = unit - factor * (unit_row * scale)
        if j in (20, 40):
            relay(j // 20)
    relay(3) if n_z > 3 else None
    pivots = jnp.where(on_diagonal, matrix, 0.0)
    left_pivot = jnp.sum(jnp.where(left, pivots, 0.0), axis=1, keepdims=True)
    right_pivot = jnp.sum(jnp.where(left, 0.0, pivots), axis=1, keepdims=True)
    l_send[...] = unit * (math.sqrt(width) * jnp.where(left, lax.rsqrt(left_pivot), lax.rsqrt(right_pivot)))
    send(l_send, l_recv, send_sem.at[20], recv_sem.at[20], sibling)
    arrived(l_recv, recv_sem.at[20])

    for i in range(2):
        for s in range(2):
            arrived(f_all.at[s, i], f_sem.at[s, i])
    for s in range(2):
        packed = jnp.where(s == c, l_send[...], l_recv[...])
        block = jnp.concatenate([jnp.where(left, packed, 0.0), jnp.where(left, 0.0, packed)], axis=0)
        high = block.astype(jnp.bfloat16)
        low = (block - high.astype(jnp.float32)).astype(jnp.bfloat16)
        for i in range(2):
            for h in range(2):
                rows = f_all[s, i, h]
                turned = jnp.dot(high, rows, preferred_element_type=jnp.float32)
                turned += jnp.dot(low, rows, preferred_element_type=jnp.float32)
                at = i * 256 + h * 128
                basis_ref[s, at : at + 128, :] = turned.T

    for d in range(1, n_z):
        source = (z + n_z - d) % n_z
        for kind, offset in ((3, 0), (4, half_rows)):
            part = piece(diag, source, offset, half_rows)
            arrived(part, w_recv.at[kind, d - 1])
            w_copy(part, part, sib_sem, sibling)
    arrived(w_all.at[0 : w_all.shape[0] // 2], sib_sem)

    top = order_ref[0]
    tile = 512
    top_inverse = inverse[top]

    def columns(step, inner):
        at = pl.multiple_of(step * tile, tile)
        product = lax.dot_general(
            cot_ref[top], w_all[pl.ds(at, tile), :], (((1,), (1,)), ((), ())),
            preferred_element_type=jnp.float32,
        )
        product = product * gain_ref[pl.ds(top, 1), pl.ds(at, tile)]
        scaled[:, pl.ds(at, tile)] = product
        unit_rows = hidden_ref[top, :, pl.ds(at, tile)].astype(jnp.float32) * top_inverse
        return inner + jnp.sum(product * unit_rows, axis=1, keepdims=True)

    inner = lax.fori_loop(0, width // tile, columns, jnp.zeros((tokens, 1), jnp.float32))
    inner_mean = inner / width

    def finish(step, carry):
        at = pl.multiple_of(step * tile, tile)
        unit_rows = hidden_ref[top, :, pl.ds(at, tile)].astype(jnp.float32) * top_inverse
        grad_ref[:, pl.ds(at, tile)] = (
            top_inverse * (scaled[:, pl.ds(at, tile)] - unit_rows * inner_mean)
        ).astype(jnp.bfloat16)
        return carry

    lax.fori_loop(0, width // tile, finish, 0)

    for copy in pending:
        copy.wait_send()

    @pl.when(y != c)
    def _():
        to_sibling.wait_send()


def fused_body(n_dp, n_fsdp, hidden, cotangent, proj_weight, norm_gain, prev_factor, factor_ranks, layer_order):
    layers, tokens, width = hidden.shape
    n_z = n_fsdp // 2
    kv = cotangent.shape[2]
    owned = width // n_fsdp
    top_weight = lax.dynamic_index_in_dim(proj_weight, layer_order[0], 0, keepdims=False)
    top_weight = top_weight.reshape(n_dp, owned // n_dp, kv)
    vmem = pl.BlockSpec(memory_space=pltpu.VMEM)
    smem = pl.BlockSpec(memory_space=pltpu.SMEM)
    half = jnp.bfloat16
    full = jnp.float32
    dma = pltpu.SemaphoreType.DMA
    return pl.pallas_call(
        functools.partial(fused_kernel, n_z),
        out_shape=(
            jax.ShapeDtypeStruct((tokens, width), half),
            jax.ShapeDtypeStruct((layers, owned, prev_factor.shape[2]), full),
        ),
        in_specs=[smem, smem] + [vmem] * 5,
        out_specs=(vmem, vmem),
        scratch_shapes=[
            pltpu.VMEM((2, 2, 2, n_z, 128, 128), full),
            pltpu.VMEM((2, 2, 2, n_z, 128, 128), half),
            pltpu.VMEM((2, 2, 2, n_z, 128, 128), half),
            pltpu.VMEM((2, 2, n_z, 128, 128), half),
            pltpu.VMEM((2, 2, n_z, 128, 128), half),
            pltpu.VMEM((2, n_z, 128, 128), half),
            pltpu.VMEM((2, n_z, 128, 128), half),
            pltpu.VMEM((2, n_z, 128, 128), full),
            pltpu.VMEM((n_z, 2, 128, 128), half),
            pltpu.VMEM((n_z, 2, 128, 128), half),
            pltpu.VMEM((2, 128, 128), half),
            pltpu.VMEM((2, 2, 2, 128, 128), half),
            pltpu.VMEM((4, 64, 128), full),
            pltpu.VMEM((8, 128), full),
            pltpu.VMEM((n_z, 64, 128), full),
            pltpu.VMEM((64, 128), full),
            pltpu.VMEM((64, 128), full),
            pltpu.VMEM((width, kv), half),
            pltpu.VMEM((tokens, width), full),
            pltpu.VMEM((2, tokens, 1), full),
            dma((24,)),
            dma((24,)),
            dma((2, 2)),
            dma((64,)),
            dma((5, n_z)),
            dma,
            dma((4,)),
        ],
        compiler_params=pltpu.CompilerParams(
            collective_id=0, has_side_effects=True, vmem_limit_bytes=60 * 1024 * 1024
        ),
    )(factor_ranks.reshape(-1), layer_order, hidden, cotangent, top_weight, norm_gain, prev_factor)


def solution(mesh):
    in_specs = (
        P(None, ("dp", "fsdp"), None),
        P(None, ("dp", "fsdp"), None),
        P(None, "fsdp", None),
        P(),
        P(),
        P(),
        P(),
    )
    out_specs = (P(("dp", "fsdp"), None), P(None, "fsdp", None))
    n_dp, n_fsdp = mesh.shape["dp"], mesh.shape["fsdp"]
    step = body
    if n_dp == 4 and n_fsdp % 2 == 0 and D // (n_dp * n_fsdp // 2) == 2 * 128:
        step = functools.partial(fused_body, n_dp, n_fsdp)
    return jax.shard_map(step, mesh=mesh, in_specs=in_specs, out_specs=out_specs, check_vma=False)
```

```python
import functools
import math

import jax
import jax.numpy as jnp
from jax import lax
from jax.experimental import pallas as pl
from jax.experimental.pallas import tpu as pltpu
from jax.sharding import PartitionSpec as P

D = 4096


def normalize(hidden_rows, gain_row):
    wide_rows = hidden_rows.astype(jnp.float32)
    inverse = lax.rsqrt(jnp.mean(wide_rows * wide_rows, axis=1, keepdims=True) + 1e-05)
    normed = (wide_rows * inverse * gain_row[None, :]).astype(jnp.bfloat16)
    return (inverse, normed)


def masked_factors(factors, rank_pair):
    rank_cols = factors.shape[1] // 2
    position = jnp.arange(2 * rank_cols)
    column = position % rank_cols
    column_limit = jnp.where(position < rank_cols, rank_pair[0], rank_pair[1])
    return jnp.where((column < column_limit)[None, :], factors, jnp.zeros_like(factors))


def project(grad_rows, kept_factor):
    head_cols = grad_rows.shape[1] // 2
    rank_cols = kept_factor.shape[1] // 2
    keys_part = jnp.dot(
        grad_rows[:, :head_cols], kept_factor[:, :rank_cols], preferred_element_type=jnp.float32
    )
    values_part = jnp.dot(
        grad_rows[:, head_cols:], kept_factor[:, rank_cols:], preferred_element_type=jnp.float32
    )
    return jnp.concatenate([keys_part, values_part], axis=1).astype(jnp.bfloat16)


def gram_pair(factor_shard):
    row_count = factor_shard.shape[0]
    rank_cols = factor_shard.shape[1] // 2
    paired = factor_shard.reshape(row_count, 2, rank_cols)
    return jnp.einsum(
        "rmi,rmj->mij",
        paired,
        paired,
        precision=lax.Precision.HIGHEST,
        preferred_element_type=jnp.float32,
    )


def orthonormal(factor_shard, gram_totals, rank_pair):
    rank_cols = factor_shard.shape[1] // 2
    column = jnp.arange(rank_cols)
    pieces = []
    for member in range(2):
        block_cols = factor_shard[:, member * rank_cols : (member + 1) * rank_cols]
        padded = gram_totals[member] + jnp.diag((column >= rank_pair[member]).astype(jnp.float32))
        lower_factor = jnp.linalg.cholesky(padded)
        pieces.append(
            lax.linalg.triangular_solve(
                lower_factor, block_cols, left_side=False, lower=True, transpose_a=True
            )
        )
    return math.sqrt(D) * jnp.concatenate(pieces, axis=1)


def body(hidden, cotangent, proj_weight, norm_gain, prev_factor, factor_ranks, layer_order):
    layer_count = hidden.shape[0]
    top_slot = layer_order[0]
    inverses = []
    shards = []
    basis_list = []
    for slot_index in range(layer_count):
        inverse, normed = normalize(hidden[slot_index], norm_gain[slot_index])
        inverses.append(inverse)
        kept_factor = masked_factors(prev_factor[slot_index], factor_ranks[slot_index])
        projected = project(cotangent[slot_index], kept_factor)
        local_rows = lax.psum_scatter(
            lax.dot_general(
                normed, projected, (((0,), (0,)), ((), ())), preferred_element_type=jnp.float32
            ),
            "fsdp",
            scatter_dimension=0,
            tiled=True,
        )
        factor_shard = lax.psum(local_rows, "dp")
        shards.append(factor_shard)
    stacked = jnp.stack([gram_pair(factor_shard) for factor_shard in shards])
    all_grams = lax.psum(stacked, "fsdp")
    basis_list = [
        orthonormal(shards[slot_index], all_grams[slot_index], factor_ranks[slot_index])
        for slot_index in range(layer_count)
    ]
    top_grads = lax.dynamic_index_in_dim(cotangent, top_slot, 0, keepdims=False)
    top_weight = lax.dynamic_index_in_dim(proj_weight, top_slot, 0, keepdims=False)
    input_grad = lax.dot_general(
        top_grads,
        lax.all_gather(top_weight, "fsdp", axis=0, tiled=True),
        (((1,), (1,)), ((), ())),
        preferred_element_type=jnp.float32,
    )
    top_inverse = lax.dynamic_index_in_dim(jnp.stack(inverses), top_slot, 0, keepdims=False)
    top_gain = lax.dynamic_index_in_dim(norm_gain, top_slot, 0, keepdims=False)
    top_hidden = lax.dynamic_index_in_dim(hidden, top_slot, 0, keepdims=False).astype(jnp.float32)
    scaled = input_grad * top_gain[None, :]
    unit_rows = top_hidden * top_inverse
    inner_mean = jnp.mean(scaled * unit_rows, axis=1, keepdims=True)
    hidden_grad = (top_inverse * (scaled - unit_rows * inner_mean)).astype(jnp.bfloat16)
    return (hidden_grad, jnp.stack(basis_list))


MESH = pl.DeviceIdType.MESH


def fused_kernel(
    n_z, ranks_ref, order_ref, hidden_ref, cot_ref, weight_ref, gain_ref, factor_ref,
    scaled_ref, rows_ref, basis_ref,
    acc, s0_send, s0_recv, s1_send, s1_recv, s2_send, s2_recv, keep2, s3_send, s3_recv,
    f_send, f_all, g_all, z_send, z_all, l_send, l_recv, w_all, inverse,
    send_sem, recv_sem, f_sem, w_send, w_recv, sib_sem, own_sem,
):
    q = lax.axis_index("dp")
    me = lax.axis_index("fsdp")
    z, c = me // 2, me % 2
    y, x = q // 2, q % 2
    n_dp = 4
    width = hidden_ref.shape[2]
    tokens = hidden_ref.shape[1]
    per_z = width // n_z
    heads = cot_ref.shape[2] // 2
    own_rows = weight_ref.shape[0]
    qrows = own_rows // 4
    half_rows = qrows // 2
    x_nbr = y * 2 + (1 - x)
    y_nbr = (1 - y) * 2 + x
    diag = (1 - y) * 2 + (1 - x)
    sibling = (q, z * 2 + (1 - c))

    def same_core(dp_index, z_index):
        return (dp_index, z_index * 2 + c)

    barrier = pltpu.get_barrier_semaphore()
    peers = [sibling]
    for k in range(1, n_dp):
        for core in range(2):
            peers.append(((q + k) % n_dp, z * 2 + core))
    for d in range(1, n_z):
        peers.append(same_core(q, (z + d) % n_z))
    for peer in peers:
        pl.semaphore_signal(barrier, inc=1, device_id=peer, device_id_type=MESH)
    pl.semaphore_wait(barrier, len(peers))

    pending = []

    def send(src, dst, ssem, rsem, target):
        copy = pltpu.make_async_remote_copy(
            src_ref=src, dst_ref=dst, send_sem=ssem, recv_sem=rsem,
            device_id=target, device_id_type=MESH,
        )
        copy.start()
        pending.append(copy)
        return copy

    def arrived(dst, rsem):
        pltpu.make_async_remote_copy(
            src_ref=dst, dst_ref=dst, send_sem=rsem, recv_sem=rsem,
            device_id=sibling, device_id_type=MESH,
        ).wait_recv()

    def piece(dp_index, z_index, offset, rows):
        start = (z_index * 2 + c) * (n_dp * qrows) + dp_index * qrows + offset
        return w_all.at[pl.ds(pl.multiple_of(start, half_rows), rows)]

    far = (2 * z) // n_z
    near = z + far * (n_z - 1 - 2 * z)

    def physical(index):
        return index + far * (n_z - 1 - 2 * index)

    def source_of(k):
        return physical(k + (k + n_z - near) // n_z)

    inside = near != 0
    guarded = []
    w_count = [0]

    def w_copy(src, dst, rsem, target, when=None):
        ssem = w_send.at[w_count[0]]
        w_count[0] += 1
        if when is None:
            send(src, dst, ssem, rsem, target)
            return
        copy = pltpu.make_async_remote_copy(
            src_ref=src, dst_ref=dst, send_sem=ssem, recv_sem=rsem,
            device_id=target, device_id_type=MESH,
        )

        @pl.when(when)
        def _():
            copy.start()

        guarded.append((when, copy))

    own_quarter = weight_ref.at[pl.ds(pl.multiple_of(q * qrows, qrows), qrows)]
    w_copy(own_quarter, piece(q, z, 0, qrows), w_recv.at[0, z], same_core(q, physical(near + 1)))
    w_copy(own_quarter, piece(q, z, 0, qrows), w_recv.at[0, z], same_core(q, physical((near + n_z - 1) % n_z)), inside)

    def along_z(k):
        source = source_of(k)
        block = piece(q, source, 0, qrows)
        arrived(block, w_recv.at[0, source])
        onward = near + 1 if k == 0 else (near + n_z - 1) % n_z
        w_copy(block, block, w_recv.at[0, source], same_core(q, physical(onward)), inside)

    def in_plane(k):
        block = piece(q, source_of(k), 0, qrows)
        w_copy(block, block, w_recv.at[1, k], same_core(x_nbr, z))
        w_copy(block, block, w_recv.at[2, k], same_core(y_nbr, z))
        w_copy(block, block, sib_sem.at[1 + k], sibling)

    def relay(k):
        source = source_of(k)
        for kind, origin, onward, offset in ((1, x_nbr, y_nbr, 0), (2, y_nbr, x_nbr, half_rows)):
            block = piece(origin, source, 0, qrows)
            arrived(block, w_recv.at[kind, k])
            part = piece(origin, source, offset, half_rows)
            w_copy(part, part, w_recv.at[2 + kind, k], same_core(onward, z))
            w_copy(block, block, sib_sem.at[1 + k], sibling)

    def last_leg(k):
        source = source_of(k)
        for kind, offset in ((3, 0), (4, half_rows)):
            part = piece(diag, source, offset, half_rows)
            arrived(part, w_recv.at[kind, k])
            w_copy(part, part, sib_sem.at[1 + k], sibling)

    top = order_ref[0]

    def gradient_columns(source, slot_sem, inner):
        arrived(w_all.at[0:own_rows], slot_sem)
        for core in range(2):
            at = pl.multiple_of((source * 2 + core) * own_rows, own_rows)
            product = lax.dot_general(
                cot_ref[top], w_all[pl.ds(at, own_rows), :], (((1,), (1,)), ((), ())),
                preferred_element_type=jnp.float32,
            )
            product = product * gain_ref[pl.ds(top, 1), pl.ds(at, own_rows)]
            scaled_ref[:, pl.ds(at, own_rows)] = product
            unit_rows = hidden_ref[top, :, pl.ds(at, own_rows)].astype(jnp.float32) * inverse[top]
            inner = inner + jnp.sum(product * unit_rows, axis=1, keepdims=True)
        return inner

    lane = lax.broadcasted_iota(jnp.int32, (1, 128), 1)

    def slot_sums(slot, store):
        limit = jnp.where(lane < 64, ranks_ref[slot, 0], ranks_ref[slot, 1])
        kept = jnp.where(lane % 64 < limit, factor_ref[slot].astype(jnp.float32), 0.0).astype(jnp.bfloat16)
        keys_part = jnp.dot(cot_ref[slot, :, :heads], kept, preferred_element_type=jnp.float32)
        values_part = jnp.dot(cot_ref[slot, :, heads:], kept, preferred_element_type=jnp.float32)
        projected = jnp.where(lane < 64, keys_part, values_part).astype(jnp.bfloat16)
        total = jnp.zeros((tokens, 1), jnp.float32)
        for part in range(n_z):
            wide = hidden_ref[slot, :, part * per_z : (part + 1) * per_z].astype(jnp.float32)
            total += jnp.sum(wide * wide, axis=1, keepdims=True)
        inv = lax.rsqrt(total / width + 1e-05)
        inverse[slot] = inv
        flipped = projected.astype(jnp.float32).T.astype(jnp.bfloat16)
        for part in range(n_z):
            cols = slice(part * per_z, (part + 1) * per_z)
            wide = hidden_ref[slot, :, cols].astype(jnp.float32)
            gain = gain_ref[pl.ds(slot, 1), cols]
            normed = (wide * inv * gain).astype(jnp.bfloat16)
            sums = jnp.dot(flipped, normed, preferred_element_type=jnp.float32)
            for yy in range(2):
                for xx in range(2):
                    for h in range(2):
                        first, second = (xx, yy) if h == 0 else (yy, xx)
                        at = (yy * 2 + xx) * 256 + h * 128
                        store(h, first, second, part, sums[:, at : at + 128])

    def store_other(h, first, second, part, block):
        s0_send[h, first, second, part] = block.astype(jnp.bfloat16)

    def store_mine(h, first, second, part, block):
        acc[h, first, second, part] = block

    slot_sums(1 - c, store_other)
    for h in range(2):
        send(s0_send.at[h], s0_recv.at[h], send_sem.at[h], recv_sem.at[h], sibling)
    slot_sums(c, store_mine)
    own_place = piece(0, z, 0, own_rows)
    own_copy = pltpu.make_async_copy(weight_ref, own_place, own_sem)
    own_copy.start()
    w_copy(weight_ref, own_place, sib_sem.at[0], sibling)

    firsts, seconds = (x, y), (y, x)
    first_nbr, second_nbr = (x_nbr, y_nbr), (y_nbr, x_nbr)
    for h in range(2):
        a = firsts[h]
        arrived(s0_recv.at[h], recv_sem.at[h])
        s1_send[h] = (acc[h, 1 - a] + s0_recv[h, 1 - a].astype(jnp.float32)).astype(jnp.bfloat16)
        send(s1_send.at[h], s1_recv.at[h], send_sem.at[2 + h], recv_sem.at[2 + h], same_core(first_nbr[h], z))
    for h in range(2):
        a = firsts[h]
        acc[h, a] = acc[h, a] + s0_recv[h, a].astype(jnp.float32)
    along_z(0)
    for h in range(2):
        a, b = firsts[h], seconds[h]
        arrived(s1_recv.at[h], recv_sem.at[2 + h])
        s2_send[h] = (acc[h, a, 1 - b] + s1_recv[h, 1 - b].astype(jnp.float32)).astype(jnp.bfloat16)
        send(s2_send.at[h], s2_recv.at[h], send_sem.at[4 + h], recv_sem.at[4 + h], same_core(second_nbr[h], z))
    for h in range(2):
        a, b = firsts[h], seconds[h]
        keep2[h] = acc[h, a, b] + s1_recv[h, b].astype(jnp.float32)
    in_plane(0)
    along_z(1)
    for h in range(2):
        arrived(s2_recv.at[h], recv_sem.at[4 + h])
        summed = keep2[h] + s2_recv[h].astype(jnp.float32)
        keep2[h] = summed
        for part in range(n_z):
            s3_send[part, h] = summed[part].astype(jnp.bfloat16)
    for d in range(1, n_z):
        to = (z + d) % n_z
        send(s3_send.at[to], s3_recv.at[z], send_sem.at[5 + d], recv_sem.at[5 + d], same_core(q, to))
    along_z(2)
    finals = [keep2[h, z] for h in range(2)]
    for d in range(1, n_z):
        source = (z + n_z - d) % n_z
        arrived(s3_recv.at[source], recv_sem.at[5 + d])
        for h in range(2):
            finals[h] = finals[h] + s3_recv[source, h].astype(jnp.float32)

    gram = jnp.zeros((128, 128), jnp.float32)
    for h in range(2):
        gram += lax.dot_general(
            finals[h], finals[h], (((1,), (1,)), ((), ())),
            precision=lax.Precision.HIGHEST, preferred_element_type=jnp.float32,
        )
    g_all[q] = jnp.where(lane < 64, gram[0:64, :], gram[64:128, :])
    for k in range(1, n_dp):
        send(g_all.at[q], g_all.at[q], send_sem.at[8 + k], recv_sem.at[8 + k], same_core((q + k) % n_dp, z))

    for h in range(2):
        f_send[h] = finals[h].astype(jnp.bfloat16)
    f_dst = f_all.at[c, x]
    for k in range(1, n_dp):
        send(f_send, f_dst, send_sem.at[12 + k], f_sem.at[c, x], ((q + k) % n_dp, z * 2 + y))
    local = pltpu.make_async_copy(f_send, f_dst, f_sem.at[c, x])
    to_sibling = pltpu.make_async_remote_copy(
        src_ref=f_send, dst_ref=f_dst, send_sem=send_sem.at[16], recv_sem=f_sem.at[c, x],
        device_id=sibling, device_id_type=MESH,
    )

    @pl.when(y == c)
    def _():
        local.start()

    @pl.when(y != c)
    def _():
        to_sibling.start()

    in_plane(1)
    in_plane(2)
    own_copy.wait()
    inner = gradient_columns(z, sib_sem.at[0], jnp.zeros((tokens, 1), jnp.float32))

    for k in range(1, n_dp):
        source = (q + n_dp - k) % n_dp
        arrived(g_all.at[source], recv_sem.at[8 + k])
    plane = g_all[0] + g_all[1] + g_all[2] + g_all[3]
    z_all[z] = plane
    for d in range(1, n_z):
        send(z_all.at[z], z_all.at[z], send_sem.at[16 + d], recv_sem.at[16 + d], same_core(q, (z + d) % n_z))
    for d in range(1, n_z):
        arrived(z_all.at[(z + n_z - d) % n_z], recv_sem.at[16 + d])
    matrix = z_all[0]
    for part in range(1, n_z):
        matrix += z_all[part]

    row = lax.broadcasted_iota(jnp.int32, (64, 128), 0)
    column = lax.broadcasted_iota(jnp.int32, (64, 128), 1)
    left = column < 64
    limit = jnp.where(left, ranks_ref[c, 0], ranks_ref[c, 1])
    on_diagonal = row == column % 64
    matrix = matrix + jnp.where(on_diagonal & (row >= limit), 1.0, 0.0)
    unit = jnp.where(on_diagonal, 1.0, 0.0)
    for j in range(64):
        pivot_row = matrix[j : j + 1, :]
        pivot = jnp.where(lane < 64, matrix[j : j + 1, j : j + 1], matrix[j : j + 1, 64 + j : 65 + j])
        scale = 1.0 / pivot
        factor = jnp.where(left, matrix[:, j : j + 1], matrix[:, 64 + j : 65 + j])
        factor = jnp.where(row > j, factor, 0.0)
        unit_row = unit[j : j + 1, :]
        matrix = matrix - factor * (pivot_row * scale)
        unit = unit - factor * (unit_row * scale)
        if j == 20:
            relay(0)
        if j == 40:
            relay(1)
    last_leg(0)
    pivots = jnp.where(on_diagonal, matrix, 0.0)
    left_pivot = jnp.sum(jnp.where(left, pivots, 0.0), axis=1, keepdims=True)
    right_pivot = jnp.sum(jnp.where(left, 0.0, pivots), axis=1, keepdims=True)
    l_send[...] = unit * (math.sqrt(width) * jnp.where(left, lax.rsqrt(left_pivot), lax.rsqrt(right_pivot)))
    send(l_send, l_recv, send_sem.at[20], recv_sem.at[20], sibling)
    arrived(l_recv, recv_sem.at[20])

    for i in range(2):
        for s in range(2):
            arrived(f_all.at[s, i], f_sem.at[s, i])
    for s in range(2):
        packed = jnp.where(s == c, l_send[...], l_recv[...])
        block = jnp.concatenate([jnp.where(left, packed, 0.0), jnp.where(left, 0.0, packed)], axis=0)
        high = block.astype(jnp.bfloat16)
        low = (block - high.astype(jnp.float32)).astype(jnp.bfloat16)
        for i in range(2):
            for h in range(2):
                rows = f_all[s, i, h]
                turned = jnp.dot(high, rows, preferred_element_type=jnp.float32)
                turned += jnp.dot(low, rows, preferred_element_type=jnp.float32)
                at = i * 256 + h * 128
                basis_ref[s, at : at + 128, :] = turned.T

    inner = gradient_columns(source_of(0), sib_sem.at[1], inner)
    relay(2)
    last_leg(1)
    inner = gradient_columns(source_of(1), sib_sem.at[2], inner)
    last_leg(2)
    inner = gradient_columns(source_of(2), sib_sem.at[3], inner)
    rows_ref[0] = jnp.broadcast_to(inner / width, (tokens, 128))
    rows_ref[1] = jnp.broadcast_to(inverse[top], (tokens, 128))

    for copy in pending:
        copy.wait_send()

    for when, copy in guarded:
        pl.when(when)(copy.wait_send)

    @pl.when(y != c)
    def _():
        to_sibling.wait_send()


def fused_body(n_dp, n_fsdp, hidden, cotangent, proj_weight, norm_gain, prev_factor, factor_ranks, layer_order):
    layers, tokens, width = hidden.shape
    n_z = n_fsdp // 2
    kv = cotangent.shape[2]
    owned = width // n_fsdp
    top_weight = lax.dynamic_index_in_dim(proj_weight, layer_order[0], 0, keepdims=False)
    vmem = pl.BlockSpec(memory_space=pltpu.VMEM)
    smem = pl.BlockSpec(memory_space=pltpu.SMEM)
    half = jnp.bfloat16
    full = jnp.float32
    dma = pltpu.SemaphoreType.DMA
    scaled, rows, basis = pl.pallas_call(
        functools.partial(fused_kernel, n_z),
        out_shape=(
            jax.ShapeDtypeStruct((tokens, width), full),
            jax.ShapeDtypeStruct((2, tokens, 128), full),
            jax.ShapeDtypeStruct((layers, owned, prev_factor.shape[2]), full),
        ),
        in_specs=[smem, smem] + [vmem] * 5,
        out_specs=(vmem, vmem, vmem),
        scratch_shapes=[
            pltpu.VMEM((2, 2, 2, n_z, 128, 128), full),
            pltpu.VMEM((2, 2, 2, n_z, 128, 128), half),
            pltpu.VMEM((2, 2, 2, n_z, 128, 128), half),
            pltpu.VMEM((2, 2, n_z, 128, 128), half),
            pltpu.VMEM((2, 2, n_z, 128, 128), half),
            pltpu.VMEM((2, n_z, 128, 128), half),
            pltpu.VMEM((2, n_z, 128, 128), half),
            pltpu.VMEM((2, n_z, 128, 128), full),
            pltpu.VMEM((n_z, 2, 128, 128), half),
            pltpu.VMEM((n_z, 2, 128, 128), half),
            pltpu.VMEM((2, 128, 128), half),
            pltpu.VMEM((2, 2, 2, 128, 128), half),
            pltpu.VMEM((4, 64, 128), full),
            pltpu.VMEM((8, 128), full),
            pltpu.VMEM((n_z, 64, 128), full),
            pltpu.VMEM((64, 128), full),
            pltpu.VMEM((64, 128), full),
            pltpu.VMEM((width, kv), half),
            pltpu.VMEM((2, tokens, 1), full),
            dma((24,)),
            dma((24,)),
            dma((2, 2)),
            dma((64,)),
            dma((5, n_z)),
            dma((4,)),
            dma,
        ],
        compiler_params=pltpu.CompilerParams(
            collective_id=0, has_side_effects=True, vmem_limit_bytes=60 * 1024 * 1024
        ),
    )(factor_ranks, layer_order, hidden, cotangent, top_weight, norm_gain, prev_factor)
    top_hidden = lax.dynamic_index_in_dim(hidden, layer_order[0], 0, keepdims=False).astype(full)
    inner_mean, top_inverse = rows[0, :, :1], rows[1, :, :1]
    hidden_grad = top_inverse * (scaled - top_hidden * top_inverse * inner_mean)
    return (hidden_grad.astype(half), basis)


def solution(mesh):
    in_specs = (
        P(None, ("dp", "fsdp"), None),
        P(None, ("dp", "fsdp"), None),
        P(None, "fsdp", None),
        P(),
        P(),
        P(),
        P(),
    )
    out_specs = (P(("dp", "fsdp"), None), P(None, "fsdp", None))
    n_dp, n_fsdp = mesh.shape["dp"], mesh.shape["fsdp"]
    step = body
    if n_dp == 4 and n_fsdp % 2 == 0 and D // (n_dp * n_fsdp // 2) == 2 * 128:
        step = functools.partial(fused_body, n_dp, n_fsdp)
    return jax.shard_map(step, mesh=mesh, in_specs=in_specs, out_specs=out_specs, check_vma=False)
```

```python
import functools
import math

import jax
import jax.numpy as jnp
from jax import lax
from jax.experimental import pallas as pl
from jax.experimental.pallas import tpu as pltpu
from jax.sharding import PartitionSpec as P

D = 4096


def normalize(hidden_rows, gain_row):
    wide_rows = hidden_rows.astype(jnp.float32)
    inverse = lax.rsqrt(jnp.mean(wide_rows * wide_rows, axis=1, keepdims=True) + 1e-05)
    normed = (wide_rows * inverse * gain_row[None, :]).astype(jnp.bfloat16)
    return (inverse, normed)


def masked_factors(factors, rank_pair):
    rank_cols = factors.shape[1] // 2
    position = jnp.arange(2 * rank_cols)
    column = position % rank_cols
    column_limit = jnp.where(position < rank_cols, rank_pair[0], rank_pair[1])
    return jnp.where((column < column_limit)[None, :], factors, jnp.zeros_like(factors))


def project(grad_rows, kept_factor):
    head_cols = grad_rows.shape[1] // 2
    rank_cols = kept_factor.shape[1] // 2
    keys_part = jnp.dot(
        grad_rows[:, :head_cols], kept_factor[:, :rank_cols], preferred_element_type=jnp.float32
    )
    values_part = jnp.dot(
        grad_rows[:, head_cols:], kept_factor[:, rank_cols:], preferred_element_type=jnp.float32
    )
    return jnp.concatenate([keys_part, values_part], axis=1).astype(jnp.bfloat16)


def gram_pair(factor_shard):
    row_count = factor_shard.shape[0]
    rank_cols = factor_shard.shape[1] // 2
    paired = factor_shard.reshape(row_count, 2, rank_cols)
    return jnp.einsum(
        "rmi,rmj->mij",
        paired,
        paired,
        precision=lax.Precision.HIGHEST,
        preferred_element_type=jnp.float32,
    )


def orthonormal(factor_shard, gram_totals, rank_pair):
    rank_cols = factor_shard.shape[1] // 2
    column = jnp.arange(rank_cols)
    pieces = []
    for member in range(2):
        block_cols = factor_shard[:, member * rank_cols : (member + 1) * rank_cols]
        padded = gram_totals[member] + jnp.diag((column >= rank_pair[member]).astype(jnp.float32))
        lower_factor = jnp.linalg.cholesky(padded)
        pieces.append(
            lax.linalg.triangular_solve(
                lower_factor, block_cols, left_side=False, lower=True, transpose_a=True
            )
        )
    return math.sqrt(D) * jnp.concatenate(pieces, axis=1)


def body(hidden, cotangent, proj_weight, norm_gain, prev_factor, factor_ranks, layer_order):
    layer_count = hidden.shape[0]
    top_slot = layer_order[0]
    inverses = []
    shards = []
    basis_list = []
    for slot_index in range(layer_count):
        inverse, normed = normalize(hidden[slot_index], norm_gain[slot_index])
        inverses.append(inverse)
        kept_factor = masked_factors(prev_factor[slot_index], factor_ranks[slot_index])
        projected = project(cotangent[slot_index], kept_factor)
        local_rows = lax.psum_scatter(
            lax.dot_general(
                normed, projected, (((0,), (0,)), ((), ())), preferred_element_type=jnp.float32
            ),
            "fsdp",
            scatter_dimension=0,
            tiled=True,
        )
        factor_shard = lax.psum(local_rows, "dp")
        shards.append(factor_shard)
    stacked = jnp.stack([gram_pair(factor_shard) for factor_shard in shards])
    all_grams = lax.psum(stacked, "fsdp")
    basis_list = [
        orthonormal(shards[slot_index], all_grams[slot_index], factor_ranks[slot_index])
        for slot_index in range(layer_count)
    ]
    top_grads = lax.dynamic_index_in_dim(cotangent, top_slot, 0, keepdims=False)
    top_weight = lax.dynamic_index_in_dim(proj_weight, top_slot, 0, keepdims=False)
    input_grad = lax.dot_general(
        top_grads,
        lax.all_gather(top_weight, "fsdp", axis=0, tiled=True),
        (((1,), (1,)), ((), ())),
        preferred_element_type=jnp.float32,
    )
    top_inverse = lax.dynamic_index_in_dim(jnp.stack(inverses), top_slot, 0, keepdims=False)
    top_gain = lax.dynamic_index_in_dim(norm_gain, top_slot, 0, keepdims=False)
    top_hidden = lax.dynamic_index_in_dim(hidden, top_slot, 0, keepdims=False).astype(jnp.float32)
    scaled = input_grad * top_gain[None, :]
    unit_rows = top_hidden * top_inverse
    inner_mean = jnp.mean(scaled * unit_rows, axis=1, keepdims=True)
    hidden_grad = (top_inverse * (scaled - unit_rows * inner_mean)).astype(jnp.bfloat16)
    return (hidden_grad, jnp.stack(basis_list))


MESH = pl.DeviceIdType.MESH


def fused_kernel(
    n_z, ranks_ref, order_ref, hidden_ref, cot_ref, weight_ref, gain_ref, factor_ref,
    scaled_ref, rows_ref, basis_ref,
    acc, s0_send, s0_recv, s1_send, s1_recv, s2_send, s2_recv, keep2, s3_send, s3_recv,
    f_send, f_all, g_all, z_send, z_all, l_send, l_recv, w_all, inverse,
    send_sem, recv_sem, f_sem, w_send, w_recv, sib_sem, own_sem,
):
    q = lax.axis_index("dp")
    me = lax.axis_index("fsdp")
    z, c = me // 2, me % 2
    y, x = q // 2, q % 2
    n_dp = 4
    width = hidden_ref.shape[2]
    tokens = hidden_ref.shape[1]
    per_z = width // n_z
    heads = cot_ref.shape[2] // 2
    own_rows = weight_ref.shape[0]
    qrows = own_rows // 4
    half_rows = qrows // 2
    x_nbr = y * 2 + (1 - x)
    y_nbr = (1 - y) * 2 + x
    diag = (1 - y) * 2 + (1 - x)
    sibling = (q, z * 2 + (1 - c))

    def same_core(dp_index, z_index):
        return (dp_index, z_index * 2 + c)

    barrier = pltpu.get_barrier_semaphore()
    peers = [sibling]
    for k in range(1, n_dp):
        for core in range(2):
            peers.append(((q + k) % n_dp, z * 2 + core))
    for d in range(1, n_z):
        peers.append(same_core(q, (z + d) % n_z))
    for peer in peers:
        pl.semaphore_signal(barrier, inc=1, device_id=peer, device_id_type=MESH)
    pl.semaphore_wait(barrier, len(peers))

    pending = []

    def send(src, dst, ssem, rsem, target):
        copy = pltpu.make_async_remote_copy(
            src_ref=src, dst_ref=dst, send_sem=ssem, recv_sem=rsem,
            device_id=target, device_id_type=MESH,
        )
        copy.start()
        pending.append(copy)
        return copy

    def arrived(dst, rsem):
        pltpu.make_async_remote_copy(
            src_ref=dst, dst_ref=dst, send_sem=rsem, recv_sem=rsem,
            device_id=sibling, device_id_type=MESH,
        ).wait_recv()

    def piece(dp_index, z_index, offset, rows):
        start = (z_index * 2 + c) * (n_dp * qrows) + dp_index * qrows + offset
        return w_all.at[pl.ds(pl.multiple_of(start, half_rows), rows)]

    far = (2 * z) // n_z
    near = z + far * (n_z - 1 - 2 * z)

    def physical(index):
        return index + far * (n_z - 1 - 2 * index)

    def source_of(k):
        return physical(k + (k + n_z - near) // n_z)

    inside = near != 0
    guarded = []
    w_count = [0]

    def w_copy(src, dst, rsem, target, when=None):
        ssem = w_send.at[w_count[0]]
        w_count[0] += 1
        if when is None:
            send(src, dst, ssem, rsem, target)
            return
        copy = pltpu.make_async_remote_copy(
            src_ref=src, dst_ref=dst, send_sem=ssem, recv_sem=rsem,
            device_id=target, device_id_type=MESH,
        )

        @pl.when(when)
        def _():
            copy.start()

        guarded.append((when, copy))

    own_quarter = weight_ref.at[pl.ds(pl.multiple_of(q * qrows, qrows), qrows)]
    w_copy(own_quarter, piece(q, z, 0, qrows), w_recv.at[0, z], same_core(q, physical(near + 1)))
    w_copy(own_quarter, piece(q, z, 0, qrows), w_recv.at[0, z], same_core(q, physical((near + n_z - 1) % n_z)), inside)

    def along_z(k):
        source = source_of(k)
        block = piece(q, source, 0, qrows)
        arrived(block, w_recv.at[0, source])
        onward = near + 1 if k == 0 else (near + n_z - 1) % n_z
        w_copy(block, block, w_recv.at[0, source], same_core(q, physical(onward)), inside)

    def in_plane(k):
        block = piece(q, source_of(k), 0, qrows)
        w_copy(block, block, w_recv.at[1, k], same_core(x_nbr, z))
        w_copy(block, block, w_recv.at[2, k], same_core(y_nbr, z))
        w_copy(block, block, sib_sem.at[1 + k], sibling)

    def relay(k):
        source = source_of(k)
        for kind, origin, onward, offset in ((1, x_nbr, y_nbr, 0), (2, y_nbr, x_nbr, half_rows)):
            block = piece(origin, source, 0, qrows)
            arrived(block, w_recv.at[kind, k])
            part = piece(origin, source, offset, half_rows)
            w_copy(part, part, w_recv.at[2 + kind, k], same_core(onward, z))
            w_copy(block, block, sib_sem.at[1 + k], sibling)

    def last_leg(k):
        source = source_of(k)
        for kind, offset in ((3, 0), (4, half_rows)):
            part = piece(diag, source, offset, half_rows)
            arrived(part, w_recv.at[kind, k])
            w_copy(part, part, sib_sem.at[1 + k], sibling)

    top = order_ref[0]

    def gradient_columns(source, slot_sem, inner):
        arrived(w_all.at[0:own_rows], slot_sem)
        for core in range(2):
            at = pl.multiple_of((source * 2 + core) * own_rows, own_rows)
            product = lax.dot_general(
                cot_ref[top], w_all[pl.ds(at, own_rows), :], (((1,), (1,)), ((), ())),
                preferred_element_type=jnp.float32,
            )
            product = product * gain_ref[pl.ds(top, 1), pl.ds(at, own_rows)]
            scaled_ref[:, pl.ds(at, own_rows)] = product
            unit_rows = hidden_ref[top, :, pl.ds(at, own_rows)].astype(jnp.float32) * inverse[top]
            inner = inner + jnp.sum(product * unit_rows, axis=1, keepdims=True)
        return inner

    lane = lax.broadcasted_iota(jnp.int32, (1, 128), 1)

    def slot_sums(slot, store):
        limit = jnp.where(lane < 64, ranks_ref[slot, 0], ranks_ref[slot, 1])
        kept = jnp.where(lane % 64 < limit, factor_ref[slot].astype(jnp.float32), 0.0).astype(jnp.bfloat16)
        keys_part = jnp.dot(cot_ref[slot, :, :heads], kept, preferred_element_type=jnp.float32)
        values_part = jnp.dot(cot_ref[slot, :, heads:], kept, preferred_element_type=jnp.float32)
        projected = jnp.where(lane < 64, keys_part, values_part).astype(jnp.bfloat16)
        total = jnp.zeros((tokens, 1), jnp.float32)
        for part in range(n_z):
            wide = hidden_ref[slot, :, part * per_z : (part + 1) * per_z].astype(jnp.float32)
            total += jnp.sum(wide * wide, axis=1, keepdims=True)
        inv = lax.rsqrt(total / width + 1e-05)
        inverse[slot] = inv
        flipped = projected.astype(jnp.float32).T.astype(jnp.bfloat16)
        for part in range(n_z):
            cols = slice(part * per_z, (part + 1) * per_z)
            wide = hidden_ref[slot, :, cols].astype(jnp.float32)
            gain = gain_ref[pl.ds(slot, 1), cols]
            normed = (wide * inv * gain).astype(jnp.bfloat16)
            sums = jnp.dot(flipped, normed, preferred_element_type=jnp.float32)
            for yy in range(2):
                for xx in range(2):
                    for h in range(2):
                        first, second = (xx, yy) if h == 0 else (yy, xx)
                        at = (yy * 2 + xx) * 256 + h * 128
                        store(h, first, second, part, sums[:, at : at + 128])

    def store_other(h, first, second, part, block):
        s0_send[h, first, second, part] = block.astype(jnp.bfloat16)

    def store_mine(h, first, second, part, block):
        acc[h, first, second, part] = block

    slot_sums(1 - c, store_other)
    for h in range(2):
        send(s0_send.at[h], s0_recv.at[h], send_sem.at[h], recv_sem.at[h], sibling)
    slot_sums(c, store_mine)
    own_place = piece(0, z, 0, own_rows)
    own_copy = pltpu.make_async_copy(weight_ref, own_place, own_sem)
    own_copy.start()
    w_copy(weight_ref, own_place, sib_sem.at[0], sibling)

    firsts, seconds = (x, y), (y, x)
    first_nbr, second_nbr = (x_nbr, y_nbr), (y_nbr, x_nbr)
    for h in range(2):
        a = firsts[h]
        arrived(s0_recv.at[h], recv_sem.at[h])
        s1_send[h] = (acc[h, 1 - a] + s0_recv[h, 1 - a].astype(jnp.float32)).astype(jnp.bfloat16)
        send(s1_send.at[h], s1_recv.at[h], send_sem.at[2 + h], recv_sem.at[2 + h], same_core(first_nbr[h], z))
    for h in range(2):
        a = firsts[h]
        acc[h, a] = acc[h, a] + s0_recv[h, a].astype(jnp.float32)
    along_z(0)
    for h in range(2):
        a, b = firsts[h], seconds[h]
        arrived(s1_recv.at[h], recv_sem.at[2 + h])
        s2_send[h] = (acc[h, a, 1 - b] + s1_recv[h, 1 - b].astype(jnp.float32)).astype(jnp.bfloat16)
        send(s2_send.at[h], s2_recv.at[h], send_sem.at[4 + h], recv_sem.at[4 + h], same_core(second_nbr[h], z))
    for h in range(2):
        a, b = firsts[h], seconds[h]
        keep2[h] = acc[h, a, b] + s1_recv[h, b].astype(jnp.float32)
    in_plane(0)
    along_z(1)
    in_plane(1)
    for h in range(2):
        arrived(s2_recv.at[h], recv_sem.at[4 + h])
        summed = keep2[h] + s2_recv[h].astype(jnp.float32)
        keep2[h] = summed
        for part in range(n_z):
            s3_send[part, h] = summed[part].astype(jnp.bfloat16)
    for d in range(1, n_z):
        to = (z + d) % n_z
        send(s3_send.at[to], s3_recv.at[z], send_sem.at[5 + d], recv_sem.at[5 + d], same_core(q, to))
    along_z(2)
    finals = [keep2[h, z] for h in range(2)]
    for d in range(1, n_z):
        source = (z + n_z - d) % n_z
        arrived(s3_recv.at[source], recv_sem.at[5 + d])
        for h in range(2):
            finals[h] = finals[h] + s3_recv[source, h].astype(jnp.float32)

    gram = jnp.zeros((128, 128), jnp.float32)
    for h in range(2):
        gram += lax.dot_general(
            finals[h], finals[h], (((1,), (1,)), ((), ())),
            precision=lax.Precision.HIGHEST, preferred_element_type=jnp.float32,
        )
    g_all[q] = jnp.where(lane < 64, gram[0:64, :], gram[64:128, :])
    for k in range(1, n_dp):
        send(g_all.at[q], g_all.at[q], send_sem.at[8 + k], recv_sem.at[8 + k], same_core((q + k) % n_dp, z))

    for h in range(2):
        f_send[h] = finals[h].astype(jnp.bfloat16)
    f_dst = f_all.at[c, x]
    for k in range(1, n_dp):
        send(f_send, f_dst, send_sem.at[12 + k], f_sem.at[c, x], ((q + k) % n_dp, z * 2 + y))
    local = pltpu.make_async_copy(f_send, f_dst, f_sem.at[c, x])
    to_sibling = pltpu.make_async_remote_copy(
        src_ref=f_send, dst_ref=f_dst, send_sem=send_sem.at[16], recv_sem=f_sem.at[c, x],
        device_id=sibling, device_id_type=MESH,
    )

    @pl.when(y == c)
    def _():
        local.start()

    @pl.when(y != c)
    def _():
        to_sibling.start()

    in_plane(2)
    relay(0)
    own_copy.wait()
    inner = gradient_columns(z, sib_sem.at[0], jnp.zeros((tokens, 1), jnp.float32))

    for k in range(1, n_dp):
        source = (q + n_dp - k) % n_dp
        arrived(g_all.at[source], recv_sem.at[8 + k])
    plane = g_all[0] + g_all[1] + g_all[2] + g_all[3]
    z_all[z] = plane
    for d in range(1, n_z):
        send(z_all.at[z], z_all.at[z], send_sem.at[16 + d], recv_sem.at[16 + d], same_core(q, (z + d) % n_z))
    for d in range(1, n_z):
        arrived(z_all.at[(z + n_z - d) % n_z], recv_sem.at[16 + d])
    matrix = z_all[0]
    for part in range(1, n_z):
        matrix += z_all[part]

    row = lax.broadcasted_iota(jnp.int32, (64, 128), 0)
    column = lax.broadcasted_iota(jnp.int32, (64, 128), 1)
    left = column < 64
    limit = jnp.where(left, ranks_ref[c, 0], ranks_ref[c, 1])
    on_diagonal = row == column % 64
    matrix = matrix + jnp.where(on_diagonal & (row >= limit), 1.0, 0.0)
    unit = jnp.where(on_diagonal, 1.0, 0.0)
    for j in range(64):
        pivot_row = matrix[j : j + 1, :]
        pivot = jnp.where(lane < 64, matrix[j : j + 1, j : j + 1], matrix[j : j + 1, 64 + j : 65 + j])
        scale = 1.0 / pivot
        factor = jnp.where(left, matrix[:, j : j + 1], matrix[:, 64 + j : 65 + j])
        factor = jnp.where(row > j, factor, 0.0)
        unit_row = unit[j : j + 1, :]
        matrix = matrix - factor * (pivot_row * scale)
        unit = unit - factor * (unit_row * scale)
        if j == 20:
            relay(1)
    pivots = jnp.where(on_diagonal, matrix, 0.0)
    left_pivot = jnp.sum(jnp.where(left, pivots, 0.0), axis=1, keepdims=True)
    right_pivot = jnp.sum(jnp.where(left, 0.0, pivots), axis=1, keepdims=True)
    l_send[...] = unit * (math.sqrt(width) * jnp.where(left, lax.rsqrt(left_pivot), lax.rsqrt(right_pivot)))
    send(l_send, l_recv, send_sem.at[20], recv_sem.at[20], sibling)
    arrived(l_recv, recv_sem.at[20])

    relay(2)
    last_leg(0)
    for i in range(2):
        for s in range(2):
            arrived(f_all.at[s, i], f_sem.at[s, i])
    for s in range(2):
        packed = jnp.where(s == c, l_send[...], l_recv[...])
        block = jnp.concatenate([jnp.where(left, packed, 0.0), jnp.where(left, 0.0, packed)], axis=0)
        high = block.astype(jnp.bfloat16)
        low = (block - high.astype(jnp.float32)).astype(jnp.bfloat16)
        for i in range(2):
            for h in range(2):
                rows = f_all[s, i, h]
                turned = jnp.dot(high, rows, preferred_element_type=jnp.float32)
                turned += jnp.dot(low, rows, preferred_element_type=jnp.float32)
                at = i * 256 + h * 128
                basis_ref[s, at : at + 128, :] = turned.T

    inner = gradient_columns(source_of(0), sib_sem.at[1], inner)
    last_leg(1)
    inner = gradient_columns(source_of(1), sib_sem.at[2], inner)
    last_leg(2)
    inner = gradient_columns(source_of(2), sib_sem.at[3], inner)
    rows_ref[0] = jnp.broadcast_to(inner / width, (tokens, 128))
    rows_ref[1] = jnp.broadcast_to(inverse[top], (tokens, 128))

    for copy in pending:
        copy.wait_send()

    for when, copy in guarded:
        pl.when(when)(copy.wait_send)

    @pl.when(y != c)
    def _():
        to_sibling.wait_send()


def fused_body(n_dp, n_fsdp, hidden, cotangent, proj_weight, norm_gain, prev_factor, factor_ranks, layer_order):
    layers, tokens, width = hidden.shape
    n_z = n_fsdp // 2
    kv = cotangent.shape[2]
    owned = width // n_fsdp
    top_weight = lax.dynamic_index_in_dim(proj_weight, layer_order[0], 0, keepdims=False)
    vmem = pl.BlockSpec(memory_space=pltpu.VMEM)
    smem = pl.BlockSpec(memory_space=pltpu.SMEM)
    half = jnp.bfloat16
    full = jnp.float32
    dma = pltpu.SemaphoreType.DMA
    scaled, rows, basis = pl.pallas_call(
        functools.partial(fused_kernel, n_z),
        out_shape=(
            jax.ShapeDtypeStruct((tokens, width), full),
            jax.ShapeDtypeStruct((2, tokens, 128), full),
            jax.ShapeDtypeStruct((layers, owned, prev_factor.shape[2]), full),
        ),
        in_specs=[smem, smem] + [vmem] * 5,
        out_specs=(vmem, vmem, vmem),
        scratch_shapes=[
            pltpu.VMEM((2, 2, 2, n_z, 128, 128), full),
            pltpu.VMEM((2, 2, 2, n_z, 128, 128), half),
            pltpu.VMEM((2, 2, 2, n_z, 128, 128), half),
            pltpu.VMEM((2, 2, n_z, 128, 128), half),
            pltpu.VMEM((2, 2, n_z, 128, 128), half),
            pltpu.VMEM((2, n_z, 128, 128), half),
            pltpu.VMEM((2, n_z, 128, 128), half),
            pltpu.VMEM((2, n_z, 128, 128), full),
            pltpu.VMEM((n_z, 2, 128, 128), half),
            pltpu.VMEM((n_z, 2, 128, 128), half),
            pltpu.VMEM((2, 128, 128), half),
            pltpu.VMEM((2, 2, 2, 128, 128), half),
            pltpu.VMEM((4, 64, 128), full),
            pltpu.VMEM((8, 128), full),
            pltpu.VMEM((n_z, 64, 128), full),
            pltpu.VMEM((64, 128), full),
            pltpu.VMEM((64, 128), full),
            pltpu.VMEM((width, kv), half),
            pltpu.VMEM((2, tokens, 1), full),
            dma((24,)),
            dma((24,)),
            dma((2, 2)),
            dma((64,)),
            dma((5, n_z)),
            dma((4,)),
            dma,
        ],
        compiler_params=pltpu.CompilerParams(
            collective_id=0, has_side_effects=True, vmem_limit_bytes=30 * 1024 * 1024
        ),
    )(factor_ranks, layer_order, hidden, cotangent, top_weight, norm_gain, prev_factor)
    top_hidden = lax.dynamic_index_in_dim(hidden, layer_order[0], 0, keepdims=False).astype(full)
    inner_mean, top_inverse = rows[0, :, :1], rows[1, :, :1]
    hidden_grad = top_inverse * (scaled - top_hidden * top_inverse * inner_mean)
    return (hidden_grad.astype(half), basis)


def solution(mesh):
    in_specs = (
        P(None, ("dp", "fsdp"), None),
        P(None, ("dp", "fsdp"), None),
        P(None, "fsdp", None),
        P(),
        P(),
        P(),
        P(),
    )
    out_specs = (P(("dp", "fsdp"), None), P(None, "fsdp", None))
    n_dp, n_fsdp = mesh.shape["dp"], mesh.shape["fsdp"]
    step = body
    if n_dp == 4 and n_fsdp % 2 == 0 and D // (n_dp * n_fsdp // 2) == 2 * 128:
        step = functools.partial(fused_body, n_dp, n_fsdp)
    return jax.shard_map(step, mesh=mesh, in_specs=in_specs, out_specs=out_specs, check_vma=False)
```

```python
import functools
import math

import jax
import jax.numpy as jnp
from jax import lax
from jax.experimental import pallas as pl
from jax.experimental.pallas import tpu as pltpu
from jax.sharding import PartitionSpec as P

D = 4096


def normalize(hidden_rows, gain_row):
    wide_rows = hidden_rows.astype(jnp.float32)
    inverse = lax.rsqrt(jnp.mean(wide_rows * wide_rows, axis=1, keepdims=True) + 1e-05)
    normed = (wide_rows * inverse * gain_row[None, :]).astype(jnp.bfloat16)
    return (inverse, normed)


def masked_factors(factors, rank_pair):
    rank_cols = factors.shape[1] // 2
    position = jnp.arange(2 * rank_cols)
    column = position % rank_cols
    column_limit = jnp.where(position < rank_cols, rank_pair[0], rank_pair[1])
    return jnp.where((column < column_limit)[None, :], factors, jnp.zeros_like(factors))


def project(grad_rows, kept_factor):
    head_cols = grad_rows.shape[1] // 2
    rank_cols = kept_factor.shape[1] // 2
    keys_part = jnp.dot(
        grad_rows[:, :head_cols], kept_factor[:, :rank_cols], preferred_element_type=jnp.float32
    )
    values_part = jnp.dot(
        grad_rows[:, head_cols:], kept_factor[:, rank_cols:], preferred_element_type=jnp.float32
    )
    return jnp.concatenate([keys_part, values_part], axis=1).astype(jnp.bfloat16)


def gram_pair(factor_shard):
    row_count = factor_shard.shape[0]
    rank_cols = factor_shard.shape[1] // 2
    paired = factor_shard.reshape(row_count, 2, rank_cols)
    return jnp.einsum(
        "rmi,rmj->mij",
        paired,
        paired,
        precision=lax.Precision.HIGHEST,
        preferred_element_type=jnp.float32,
    )


def orthonormal(factor_shard, gram_totals, rank_pair):
    rank_cols = factor_shard.shape[1] // 2
    column = jnp.arange(rank_cols)
    pieces = []
    for member in range(2):
        block_cols = factor_shard[:, member * rank_cols : (member + 1) * rank_cols]
        padded = gram_totals[member] + jnp.diag((column >= rank_pair[member]).astype(jnp.float32))
        lower_factor = jnp.linalg.cholesky(padded)
        pieces.append(
            lax.linalg.triangular_solve(
                lower_factor, block_cols, left_side=False, lower=True, transpose_a=True
            )
        )
    return math.sqrt(D) * jnp.concatenate(pieces, axis=1)


def body(hidden, cotangent, proj_weight, norm_gain, prev_factor, factor_ranks, layer_order):
    layer_count = hidden.shape[0]
    top_slot = layer_order[0]
    inverses = []
    shards = []
    basis_list = []
    for slot_index in range(layer_count):
        inverse, normed = normalize(hidden[slot_index], norm_gain[slot_index])
        inverses.append(inverse)
        kept_factor = masked_factors(prev_factor[slot_index], factor_ranks[slot_index])
        projected = project(cotangent[slot_index], kept_factor)
        local_rows = lax.psum_scatter(
            lax.dot_general(
                normed, projected, (((0,), (0,)), ((), ())), preferred_element_type=jnp.float32
            ),
            "fsdp",
            scatter_dimension=0,
            tiled=True,
        )
        factor_shard = lax.psum(local_rows, "dp")
        shards.append(factor_shard)
    stacked = jnp.stack([gram_pair(factor_shard) for factor_shard in shards])
    all_grams = lax.psum(stacked, "fsdp")
    basis_list = [
        orthonormal(shards[slot_index], all_grams[slot_index], factor_ranks[slot_index])
        for slot_index in range(layer_count)
    ]
    top_grads = lax.dynamic_index_in_dim(cotangent, top_slot, 0, keepdims=False)
    top_weight = lax.dynamic_index_in_dim(proj_weight, top_slot, 0, keepdims=False)
    input_grad = lax.dot_general(
        top_grads,
        lax.all_gather(top_weight, "fsdp", axis=0, tiled=True),
        (((1,), (1,)), ((), ())),
        preferred_element_type=jnp.float32,
    )
    top_inverse = lax.dynamic_index_in_dim(jnp.stack(inverses), top_slot, 0, keepdims=False)
    top_gain = lax.dynamic_index_in_dim(norm_gain, top_slot, 0, keepdims=False)
    top_hidden = lax.dynamic_index_in_dim(hidden, top_slot, 0, keepdims=False).astype(jnp.float32)
    scaled = input_grad * top_gain[None, :]
    unit_rows = top_hidden * top_inverse
    inner_mean = jnp.mean(scaled * unit_rows, axis=1, keepdims=True)
    hidden_grad = (top_inverse * (scaled - unit_rows * inner_mean)).astype(jnp.bfloat16)
    return (hidden_grad, jnp.stack(basis_list))


MESH = pl.DeviceIdType.MESH


def fused_kernel(
    n_z, ranks_ref, order_ref, hidden_ref, cot_ref, weight_ref, gain_ref, factor_ref,
    grad_ref, basis_ref,
    acc, s0_send, s0_recv, s1_send, s1_recv, s2_send, s2_recv, keep2, s3_send, s3_recv,
    f_send, f_all, g_all, z_send, z_all, l_send, l_recv, w_all, scaled, inverse,
    send_sem, recv_sem, f_sem, w_send, w_recv, sib_sem, own_sem,
):
    q = lax.axis_index("dp")
    me = lax.axis_index("fsdp")
    z, c = me // 2, me % 2
    y, x = q // 2, q % 2
    n_dp = 4
    width = hidden_ref.shape[2]
    tokens = hidden_ref.shape[1]
    per_z = width // n_z
    heads = cot_ref.shape[2] // 2
    own_rows = weight_ref.shape[0]
    qrows = own_rows // 4
    half_rows = qrows // 2
    x_nbr = y * 2 + (1 - x)
    y_nbr = (1 - y) * 2 + x
    diag = (1 - y) * 2 + (1 - x)
    sibling = (q, z * 2 + (1 - c))

    def same_core(dp_index, z_index):
        return (dp_index, z_index * 2 + c)

    barrier = pltpu.get_barrier_semaphore()
    peers = [sibling]
    for k in range(1, n_dp):
        for core in range(2):
            peers.append(((q + k) % n_dp, z * 2 + core))
    for d in range(1, n_z):
        peers.append(same_core(q, (z + d) % n_z))
    for peer in peers:
        pl.semaphore_signal(barrier, inc=1, device_id=peer, device_id_type=MESH)
    pl.semaphore_wait(barrier, len(peers))

    pending = []

    def send(src, dst, ssem, rsem, target):
        copy = pltpu.make_async_remote_copy(
            src_ref=src, dst_ref=dst, send_sem=ssem, recv_sem=rsem,
            device_id=target, device_id_type=MESH,
        )
        copy.start()
        pending.append(copy)
        return copy

    def arrived(dst, rsem):
        pltpu.make_async_remote_copy(
            src_ref=dst, dst_ref=dst, send_sem=rsem, recv_sem=rsem,
            device_id=sibling, device_id_type=MESH,
        ).wait_recv()

    def piece(dp_index, z_index, offset, rows):
        start = (z_index * 2 + c) * (n_dp * qrows) + dp_index * qrows + offset
        return w_all.at[pl.ds(pl.multiple_of(start, half_rows), rows)]

    far = (2 * z) // n_z
    near = z + far * (n_z - 1 - 2 * z)

    def physical(index):
        return index + far * (n_z - 1 - 2 * index)

    def source_of(k):
        return physical(k + (k + n_z - near) // n_z)

    inside = near != 0
    guarded = []
    w_count = [0]

    def w_copy(src, dst, rsem, target, when=None):
        ssem = w_send.at[w_count[0]]
        w_count[0] += 1
        if when is None:
            send(src, dst, ssem, rsem, target)
            return
        copy = pltpu.make_async_remote_copy(
            src_ref=src, dst_ref=dst, send_sem=ssem, recv_sem=rsem,
            device_id=target, device_id_type=MESH,
        )

        @pl.when(when)
        def _():
            copy.start()

        guarded.append((when, copy))

    own_quarter = weight_ref.at[pl.ds(pl.multiple_of(q * qrows, qrows), qrows)]
    w_copy(own_quarter, piece(q, z, 0, qrows), w_recv.at[0, z], same_core(q, physical(near + 1)))
    w_copy(own_quarter, piece(q, z, 0, qrows), w_recv.at[0, z], same_core(q, physical((near + n_z - 1) % n_z)), inside)

    def along_z(k):
        source = source_of(k)
        block = piece(q, source, 0, qrows)
        arrived(block, w_recv.at[0, source])
        onward = near + 1 if k == 0 else (near + n_z - 1) % n_z
        w_copy(block, block, w_recv.at[0, source], same_core(q, physical(onward)), inside)

    def in_plane(k):
        block = piece(q, source_of(k), 0, qrows)
        w_copy(block, block, w_recv.at[1, k], same_core(x_nbr, z))
        w_copy(block, block, w_recv.at[2, k], same_core(y_nbr, z))
        w_copy(block, block, sib_sem.at[1 + k], sibling)

    def relay(k):
        source = source_of(k)
        for kind, origin, onward, offset in ((1, x_nbr, y_nbr, 0), (2, y_nbr, x_nbr, half_rows)):
            block = piece(origin, source, 0, qrows)
            arrived(block, w_recv.at[kind, k])
            part = piece(origin, source, offset, half_rows)
            w_copy(part, part, w_recv.at[2 + kind, k], same_core(onward, z))
            w_copy(block, block, sib_sem.at[1 + k], sibling)

    def last_leg(k):
        source = source_of(k)
        for kind, offset in ((3, 0), (4, half_rows)):
            part = piece(diag, source, offset, half_rows)
            arrived(part, w_recv.at[kind, k])
            w_copy(part, part, sib_sem.at[1 + k], sibling)

    top = order_ref[0]

    def gradient_columns(source, slot_sem, inner):
        arrived(w_all.at[0:own_rows], slot_sem)
        for core in range(2):
            at = pl.multiple_of((source * 2 + core) * own_rows, own_rows)
            product = lax.dot_general(
                cot_ref[top], w_all[pl.ds(at, own_rows), :], (((1,), (1,)), ((), ())),
                preferred_element_type=jnp.float32,
            )
            product = product * gain_ref[pl.ds(top, 1), pl.ds(at, own_rows)]
            scaled[:, pl.ds(at, own_rows)] = product
            unit_rows = hidden_ref[top, :, pl.ds(at, own_rows)].astype(jnp.float32) * inverse[top]
            inner = inner + jnp.sum(product * unit_rows, axis=1, keepdims=True)
        return inner

    lane = lax.broadcasted_iota(jnp.int32, (1, 128), 1)

    def slot_sums(slot, store):
        limit = jnp.where(lane < 64, ranks_ref[slot, 0], ranks_ref[slot, 1])
        kept = jnp.where(lane % 64 < limit, factor_ref[slot].astype(jnp.float32), 0.0).astype(jnp.bfloat16)
        keys_part = jnp.dot(cot_ref[slot, :, :heads], kept, preferred_element_type=jnp.float32)
        values_part = jnp.dot(cot_ref[slot, :, heads:], kept, preferred_element_type=jnp.float32)
        projected = jnp.where(lane < 64, keys_part, values_part).astype(jnp.bfloat16)
        total = jnp.zeros((tokens, 1), jnp.float32)
        for part in range(n_z):
            wide = hidden_ref[slot, :, part * per_z : (part + 1) * per_z].astype(jnp.float32)
            total += jnp.sum(wide * wide, axis=1, keepdims=True)
        inv = lax.rsqrt(total / width + 1e-05)
        inverse[slot] = inv
        flipped = projected.astype(jnp.float32).T.astype(jnp.bfloat16)
        for part in range(n_z):
            cols = slice(part * per_z, (part + 1) * per_z)
            wide = hidden_ref[slot, :, cols].astype(jnp.float32)
            gain = gain_ref[pl.ds(slot, 1), cols]
            normed = (wide * inv * gain).astype(jnp.bfloat16)
            sums = jnp.dot(flipped, normed, preferred_element_type=jnp.float32)
            for yy in range(2):
                for xx in range(2):
                    for h in range(2):
                        first, second = (xx, yy) if h == 0 else (yy, xx)
                        at = (yy * 2 + xx) * 256 + h * 128
                        store(h, first, second, part, sums[:, at : at + 128])

    def store_other(h, first, second, part, block):
        s0_send[h, first, second, part] = block.astype(jnp.bfloat16)

    def store_mine(h, first, second, part, block):
        acc[h, first, second, part] = block

    slot_sums(1 - c, store_other)
    for h in range(2):
        send(s0_send.at[h], s0_recv.at[h], send_sem.at[h], recv_sem.at[h], sibling)
    slot_sums(c, store_mine)
    own_place = piece(0, z, 0, own_rows)
    own_copy = pltpu.make_async_copy(weight_ref, own_place, own_sem)
    own_copy.start()
    w_copy(weight_ref, own_place, sib_sem.at[0], sibling)

    firsts, seconds = (x, y), (y, x)
    first_nbr, second_nbr = (x_nbr, y_nbr), (y_nbr, x_nbr)
    for h in range(2):
        a = firsts[h]
        arrived(s0_recv.at[h], recv_sem.at[h])
        s1_send[h] = (acc[h, 1 - a] + s0_recv[h, 1 - a].astype(jnp.float32)).astype(jnp.bfloat16)
        send(s1_send.at[h], s1_recv.at[h], send_sem.at[2 + h], recv_sem.at[2 + h], same_core(first_nbr[h], z))
    for h in range(2):
        a = firsts[h]
        acc[h, a] = acc[h, a] + s0_recv[h, a].astype(jnp.float32)
    along_z(0)
    for h in range(2):
        a, b = firsts[h], seconds[h]
        arrived(s1_recv.at[h], recv_sem.at[2 + h])
        s2_send[h] = (acc[h, a, 1 - b] + s1_recv[h, 1 - b].astype(jnp.float32)).astype(jnp.bfloat16)
        send(s2_send.at[h], s2_recv.at[h], send_sem.at[4 + h], recv_sem.at[4 + h], same_core(second_nbr[h], z))
    for h in range(2):
        a, b = firsts[h], seconds[h]
        keep2[h] = acc[h, a, b] + s1_recv[h, b].astype(jnp.float32)
    in_plane(0)
    along_z(1)
    in_plane(1)
    for h in range(2):
        arrived(s2_recv.at[h], recv_sem.at[4 + h])
        summed = keep2[h] + s2_recv[h].astype(jnp.float32)
        keep2[h] = summed
        for part in range(n_z):
            s3_send[part, h] = summed[part].astype(jnp.bfloat16)
    for d in range(1, n_z):
        to = (z + d) % n_z
        send(s3_send.at[to], s3_recv.at[z], send_sem.at[5 + d], recv_sem.at[5 + d], same_core(q, to))
    along_z(2)
    finals = [keep2[h, z] for h in range(2)]
    for d in range(1, n_z):
        source = (z + n_z - d) % n_z
        arrived(s3_recv.at[source], recv_sem.at[5 + d])
        for h in range(2):
            finals[h] = finals[h] + s3_recv[source, h].astype(jnp.float32)

    gram = jnp.zeros((128, 128), jnp.float32)
    for h in range(2):
        gram += lax.dot_general(
            finals[h], finals[h], (((1,), (1,)), ((), ())),
            precision=lax.Precision.HIGHEST, preferred_element_type=jnp.float32,
        )
    g_all[q] = jnp.where(lane < 64, gram[0:64, :], gram[64:128, :])
    for k in range(1, n_dp):
        send(g_all.at[q], g_all.at[q], send_sem.at[8 + k], recv_sem.at[8 + k], same_core((q + k) % n_dp, z))

    for h in range(2):
        f_send[h] = finals[h].astype(jnp.bfloat16)
    f_dst = f_all.at[c, x]
    for k in range(1, n_dp):
        send(f_send, f_dst, send_sem.at[12 + k], f_sem.at[c, x], ((q + k) % n_dp, z * 2 + y))
    local = pltpu.make_async_copy(f_send, f_dst, f_sem.at[c, x])
    to_sibling = pltpu.make_async_remote_copy(
        src_ref=f_send, dst_ref=f_dst, send_sem=send_sem.at[16], recv_sem=f_sem.at[c, x],
        device_id=sibling, device_id_type=MESH,
    )

    @pl.when(y == c)
    def _():
        local.start()

    @pl.when(y != c)
    def _():
        to_sibling.start()

    in_plane(2)
    relay(0)
    own_copy.wait()
    inner = gradient_columns(z, sib_sem.at[0], jnp.zeros((tokens, 1), jnp.float32))

    for k in range(1, n_dp):
        source = (q + n_dp - k) % n_dp
        arrived(g_all.at[source], recv_sem.at[8 + k])
    plane = g_all[0] + g_all[1] + g_all[2] + g_all[3]
    z_all[z] = plane
    for d in range(1, n_z):
        send(z_all.at[z], z_all.at[z], send_sem.at[16 + d], recv_sem.at[16 + d], same_core(q, (z + d) % n_z))
    for d in range(1, n_z):
        arrived(z_all.at[(z + n_z - d) % n_z], recv_sem.at[16 + d])
    matrix = z_all[0]
    for part in range(1, n_z):
        matrix += z_all[part]

    row = lax.broadcasted_iota(jnp.int32, (64, 128), 0)
    column = lax.broadcasted_iota(jnp.int32, (64, 128), 1)
    left = column < 64
    limit = jnp.where(left, ranks_ref[c, 0], ranks_ref[c, 1])
    on_diagonal = row == column % 64
    matrix = matrix + jnp.where(on_diagonal & (row >= limit), 1.0, 0.0)
    unit = jnp.where(on_diagonal, 1.0, 0.0)
    for j in range(64):
        pivot_row = matrix[j : j + 1, :]
        pivot = jnp.where(lane < 64, matrix[j : j + 1, j : j + 1], matrix[j : j + 1, 64 + j : 65 + j])
        scale = 1.0 / pivot
        factor = jnp.where(left, matrix[:, j : j + 1], matrix[:, 64 + j : 65 + j])
        factor = jnp.where(row > j, factor, 0.0)
        unit_row = unit[j : j + 1, :]
        matrix = matrix - factor * (pivot_row * scale)
        unit = unit - factor * (unit_row * scale)
        if j == 20:
            relay(1)
    pivots = jnp.where(on_diagonal, matrix, 0.0)
    left_pivot = jnp.sum(jnp.where(left, pivots, 0.0), axis=1, keepdims=True)
    right_pivot = jnp.sum(jnp.where(left, 0.0, pivots), axis=1, keepdims=True)
    l_send[...] = unit * (math.sqrt(width) * jnp.where(left, lax.rsqrt(left_pivot), lax.rsqrt(right_pivot)))
    send(l_send, l_recv, send_sem.at[20], recv_sem.at[20], sibling)
    arrived(l_recv, recv_sem.at[20])

    relay(2)
    last_leg(0)
    for i in range(2):
        for s in range(2):
            arrived(f_all.at[s, i], f_sem.at[s, i])
    for s in range(2):
        packed = jnp.where(s == c, l_send[...], l_recv[...])
        block = jnp.concatenate([jnp.where(left, packed, 0.0), jnp.where(left, 0.0, packed)], axis=0)
        high = block.astype(jnp.bfloat16)
        low = (block - high.astype(jnp.float32)).astype(jnp.bfloat16)
        for i in range(2):
            for h in range(2):
                rows = f_all[s, i, h]
                turned = jnp.dot(high, rows, preferred_element_type=jnp.float32)
                turned += jnp.dot(low, rows, preferred_element_type=jnp.float32)
                at = i * 256 + h * 128
                basis_ref[s, at : at + 128, :] = turned.T

    inner = gradient_columns(source_of(0), sib_sem.at[1], inner)
    last_leg(1)
    inner = gradient_columns(source_of(1), sib_sem.at[2], inner)
    last_leg(2)
    inner = gradient_columns(source_of(2), sib_sem.at[3], inner)
    inner_mean = inner / width

    def finish(step, carry):
        at = pl.multiple_of(step * own_rows, own_rows)
        unit_rows = hidden_ref[top, :, pl.ds(at, own_rows)].astype(jnp.float32) * inverse[top]
        grad_ref[:, pl.ds(at, own_rows)] = (
            inverse[top] * (scaled[:, pl.ds(at, own_rows)] - unit_rows * inner_mean)
        ).astype(jnp.bfloat16)
        return carry

    lax.fori_loop(0, width // own_rows, finish, 0)

    for copy in pending:
        copy.wait_send()

    for when, copy in guarded:
        pl.when(when)(copy.wait_send)

    @pl.when(y != c)
    def _():
        to_sibling.wait_send()


def fused_body(n_dp, n_fsdp, hidden, cotangent, proj_weight, norm_gain, prev_factor, factor_ranks, layer_order):
    layers, tokens, width = hidden.shape
    n_z = n_fsdp // 2
    kv = cotangent.shape[2]
    owned = width // n_fsdp
    top_weight = lax.dynamic_index_in_dim(proj_weight, layer_order[0], 0, keepdims=False)
    vmem = pl.BlockSpec(memory_space=pltpu.VMEM)
    smem = pl.BlockSpec(memory_space=pltpu.SMEM)
    half = jnp.bfloat16
    full = jnp.float32
    dma = pltpu.SemaphoreType.DMA
    return pl.pallas_call(
        functools.partial(fused_kernel, n_z),
        out_shape=(
            jax.ShapeDtypeStruct((tokens, width), half),
            jax.ShapeDtypeStruct((layers, owned, prev_factor.shape[2]), full),
        ),
        in_specs=[smem, smem] + [vmem] * 5,
        out_specs=(vmem, vmem),
        scratch_shapes=[
            pltpu.VMEM((2, 2, 2, n_z, 128, 128), full),
            pltpu.VMEM((2, 2, 2, n_z, 128, 128), half),
            pltpu.VMEM((2, 2, 2, n_z, 128, 128), half),
            pltpu.VMEM((2, 2, n_z, 128, 128), half),
            pltpu.VMEM((2, 2, n_z, 128, 128), half),
            pltpu.VMEM((2, n_z, 128, 128), half),
            pltpu.VMEM((2, n_z, 128, 128), half),
            pltpu.VMEM((2, n_z, 128, 128), full),
            pltpu.VMEM((n_z, 2, 128, 128), half),
            pltpu.VMEM((n_z, 2, 128, 128), half),
            pltpu.VMEM((2, 128, 128), half),
            pltpu.VMEM((2, 2, 2, 128, 128), half),
            pltpu.VMEM((4, 64, 128), full),
            pltpu.VMEM((8, 128), full),
            pltpu.VMEM((n_z, 64, 128), full),
            pltpu.VMEM((64, 128), full),
            pltpu.VMEM((64, 128), full),
            pltpu.VMEM((width, kv), half),
            pltpu.VMEM((tokens, width), full),
            pltpu.VMEM((2, tokens, 1), full),
            dma((24,)),
            dma((24,)),
            dma((2, 2)),
            dma((64,)),
            dma((5, n_z)),
            dma((4,)),
            dma,
        ],
        compiler_params=pltpu.CompilerParams(
            collective_id=0, has_side_effects=True, vmem_limit_bytes=30 * 1024 * 1024
        ),
    )(factor_ranks, layer_order, hidden, cotangent, top_weight, norm_gain, prev_factor)


def solution(mesh):
    in_specs = (
        P(None, ("dp", "fsdp"), None),
        P(None, ("dp", "fsdp"), None),
        P(None, "fsdp", None),
        P(),
        P(),
        P(),
        P(),
    )
    out_specs = (P(("dp", "fsdp"), None), P(None, "fsdp", None))
    n_dp, n_fsdp = mesh.shape["dp"], mesh.shape["fsdp"]
    step = body
    if n_dp == 4 and n_fsdp % 2 == 0 and D // (n_dp * n_fsdp // 2) == 2 * 128:
        step = functools.partial(fused_body, n_dp, n_fsdp)
    return jax.shard_map(step, mesh=mesh, in_specs=in_specs, out_specs=out_specs, check_vma=False)
```
